32 devices in a mesh: wide: 16 (over z, y, x), narrow: 2 (over core).
Axes of the slice: x: 2, y: 2, z: 4, core: 2. Of those that a mesh axis runs over, the one named last changes fastest.
Arguments:
- grads: bfloat16 [14, 512, 2048], P(None, 'wide', 'narrow'), may hold values from -200 to 200
- momentum: float32 [14, 512, 2048], P(None, 'wide', 'narrow'), may hold values from -400 to 400
- owners: int32 [14], replicated, may hold values from 0 to 15, as said below
- norm_grads: float32 [28, 2048], P('narrow', 'wide'), may hold values from -6 to 6
- norm_params: float32 [28, 2048], P('narrow', 'wide'), may hold values from 0.5 to 1.5
- adam_m: float32 [28, 2048], P('narrow', 'wide'), may hold values from -4 to 4
- adam_v: float32 [28, 2048], P('narrow', 'wide'), may hold values from 0.1 to 4
Outputs:
- muon_update: bfloat16 [14, 512, 2048], P(None, 'wide', 'narrow')
- momentum_new: float32 [14, 512, 2048], P(None, 'wide', 'narrow')
- owner_load: float32 [16], P('wide')
- norm_params_new: float32 [28, 2048], P('narrow', 'wide')
- adam_m_new: float32 [28, 2048], P('narrow', 'wide')
- adam_v_new: float32 [28, 2048], P('narrow', 'wide')
The draws below stay inside these ranges and needn't reach their ends.
Inputs may be any that keep to these rules, and one draw needn't show every extreme that they name: `owners`: each of the 16 groups owns at most 2 matrices, and some group owns exactly 2.
All inputs are finite; a program needn't handle non-finite values.
Results may differ from the reference program's by a relative error of at most 0.014.
Values may be sent and summed in bfloat16 or wider, within the bound.
A program may use at most 64 MiB of HBM per device.

```python
import math
import jax
import jax.numpy as jnp
from jax import lax

D = 2048
KV_OUT = 512
ITERS = 2
CAP = 2
GROUPS = 16
MATS = 14
NVEC = 28
N_NARROW = 2


def field_draw(key, salt):
    key = jax.random.fold_in(key, salt)
    key_base, key_rows, key_cols = jax.random.split(key, 3)
    shape = (MATS, KV_OUT, D)
    row_place = jnp.arange(KV_OUT, dtype=jnp.float32) / KV_OUT
    col_place = jnp.arange(D, dtype=jnp.float32) / D
    row_scale = jnp.exp(jax.random.uniform(key_rows, (MATS, KV_OUT, 1), minval=0.0, maxval=2.3026))
    col_scale = jnp.exp(jax.random.uniform(key_cols, (MATS, 1, D), minval=0.0, maxval=2.3026))
    base = jnp.clip(jax.random.normal(key_base, shape), -5.0, 5.0)
    trend = (1.0 + 0.8 * row_place)[None, :, None] * (1.0 + 0.8 * col_place)[None, None, :]
    factor = 0.05
    return base * row_scale * col_scale * trend * factor


def draw_grads(key, part):
    return field_draw(key, 11).astype(jnp.bfloat16)


def draw_momentum(key, part):
    return (2.0 * field_draw(key, 23)).astype(jnp.float32)


def draw_owners(key, part):
    key = jax.random.fold_in(key, 37)
    slot_total = GROUPS * CAP
    places = jnp.arange(slot_total, dtype=jnp.int32)
    order = jax.random.permutation(key, slot_total).astype(jnp.int32)
    first_group = order[0] // CAP
    for member in range(1, CAP):
        target = first_group * CAP + (order[0] % CAP + member) % CAP
        where_target = jnp.argmax((order == target).astype(jnp.int32)).astype(jnp.int32)
        displaced = order[member]
        order = jnp.where(places == where_target, displaced, order)
        order = jnp.where(places == member, target, order)
    return (order[:MATS] // CAP).astype(jnp.int32)


def levels(own_key, dims, cuts, smallest, high):
    loudness, own = 1.0, jax.random.fold_in(own_key, 6)
    for position, shards_of in cuts:
        draws = jnp.exp(jax.random.uniform(jax.random.fold_in(own, position), (shards_of,), jnp.float32, smallest / len(cuts), high / len(cuts)))
        loudness = loudness * jnp.repeat(draws, dims[position] // shards_of).reshape([-1 if axis == position else 1 for axis in range(len(dims))])
    return loudness


def scatter_about(key, shape, spread, limit, shards=(), held_as=jnp.bfloat16):
    factor_of = levels(key, shape, shards, -0.22, 0.18) if shards else 1.0
    values = jax.random.normal(key, shape, jnp.float32) * spread * factor_of
    return jnp.minimum(jnp.maximum(values, -limit), limit).astype(held_as)


def setup_inputs(seed: int = 0) -> dict:
    keys = jax.random.split(jax.random.key(seed), 8)
    return {
        "grads": draw_grads(jax.random.fold_in(keys[7], 71), 0),
        "momentum": draw_momentum(jax.random.fold_in(keys[7], 71), 0),
        "owners": draw_owners(jax.random.fold_in(keys[7], 71), 0),
        "norm_grads": scatter_about(keys[3], (NVEC, D), 1.0, 6.0, ((0, 2), (1, 16)), jnp.float32),
        "norm_params": jnp.clip(1.0 + 0.1 * jax.random.normal(keys[4], (NVEC, D), jnp.float32), 0.5, 1.5),
        "adam_m": scatter_about(keys[5], (NVEC, D), 0.3, 4.0, ((0, 2), (1, 16)), jnp.float32),
        "adam_v": jnp.clip(jnp.exp(math.log(4.0) - 3.6888794 * jax.random.uniform(keys[6], (NVEC, D), jnp.float32) ** levels(keys[6], (NVEC, D), ((0, 2), (1, 16)), -0.2, 0.2)), 0.1, 4.0),
    }


coef_a = 3.4445
coef_b = -4.775
coef_c = 2.0315
muon_beta = 0.95
norm_eps = 1e-07
adam_first = 0.9
adam_second = 0.95
adam_rate = 0.02
adam_eps = 1e-08
first_fix = 1.0 - 0.9 ** 10
second_fix = 1.0 - 0.95 ** 10

def orthogonalize_one(direction):
    fro_norm = jnp.sqrt(jnp.sum(direction * direction))
    current = (direction / (fro_norm + norm_eps)).astype(jnp.bfloat16)
    result = current.astype(jnp.float32)
    for iteration in range(ITERS):
        pieces = current.astype(jnp.float32).reshape(KV_OUT, N_NARROW, D // N_NARROW)
        partial_value = jnp.einsum('mjk,njk->jmn', pieces, pieces)
        rounded = lax.optimization_barrier(partial_value.astype(jnp.bfloat16))
        gram_sum = lax.optimization_barrier(jnp.sum(rounded.astype(jnp.float32), axis=0)).astype(jnp.bfloat16)
        square = jnp.dot(gram_sum, gram_sum, preferred_element_type=jnp.float32)
        polynomial = (coef_b * gram_sum.astype(jnp.float32) + coef_c * square).astype(jnp.bfloat16)
        result = coef_a * current.astype(jnp.float32) + jnp.dot(polynomial, current, preferred_element_type=jnp.float32)
        if iteration + 1 < ITERS:
            current = result.astype(jnp.bfloat16)
    update = (math.sqrt(D) * result).astype(jnp.bfloat16)
    mean_square = jnp.mean(update.astype(jnp.float32) * update.astype(jnp.float32))
    return (update, mean_square)

def reference(grads, momentum, owners, norm_grads, norm_params, adam_m, adam_v):
    grad_values = grads.astype(jnp.float32)
    momentum_new = muon_beta * momentum + grad_values
    direction = grad_values + muon_beta * momentum_new
    muon_update, mean_squares = lax.map(orthogonalize_one, direction)
    group_ids = jnp.arange(GROUPS, dtype=jnp.int32)
    owner_load = lax.optimization_barrier(jnp.sum(jnp.where(owners[None, :] == group_ids[:, None], mean_squares[None, :], 0.0), axis=1))
    adam_m_new = adam_first * adam_m + (1.0 - adam_first) * norm_grads
    adam_v_new = adam_second * adam_v + (1.0 - adam_second) * norm_grads * norm_grads
    corrected = adam_m_new / first_fix / (jnp.sqrt(adam_v_new / second_fix) + adam_eps)
    norm_params_new = norm_params - adam_rate * corrected
    return (muon_update, momentum_new, owner_load, norm_params_new, adam_m_new, adam_v_new)
```

```python
import functools
import math

import jax
import jax.numpy as jnp
from jax import lax
from jax.experimental import pallas as pl
from jax.experimental.pallas import tpu as pltpu
from jax.sharding import PartitionSpec as P

D = 2048
KV_OUT = 512

coef_a = 3.4445
coef_b = -4.775
coef_c = 2.0315
muon_beta = 0.95
norm_eps = 1e-07
adam_first = 0.9
adam_second = 0.95
adam_rate = 0.02
adam_eps = 1e-08
first_fix = 1.0 - 0.9**10
second_fix = 1.0 - 0.95**10

MESH = pl.DeviceIdType.MESH
BF16 = jnp.bfloat16
F32 = jnp.float32


def mul(left, right):
    return jnp.dot(left, right, preferred_element_type=F32)


def kernel(
    groups, parts, mats, chunks,
    owners_hbm, grads_hbm, momentum_hbm,
    update, momentum_new, owner_load,
    dirs, blocks, results, grams, traces, halves, load_tile, loads, fresh, ident,
    dir_send, dir_recv, res_send, res_recv, gram_send, gram_recv,
    trace_send, trace_recv, half_send, half_recv, load_send, load_recv, own_sem, mom_sem,
    owners, grads, momentum, owners_sem, grads_sem, momentum_sem,
):
    me = lax.axis_index("wide")
    part = lax.axis_index("narrow")
    rows, cols = dirs.shape[1], dirs.shape[2]
    half = groups // 2
    inner = half // 2
    singles = half
    doubles = mats - singles
    upper = lax.div(me, half)

    def single_owner(matrix):
        return inner + matrix

    def double_owner(index, side):
        return jnp.where(side == 0, index, groups - 1 - index)

    my_double = jnp.where(upper == 0, me, groups - 1 - me)
    has_single = (me >= inner) & (me < inner + singles)
    has_double = my_double < doubles

    def group_at(step):
        return lax.rem(me + step, groups)

    def elsewhere(group, body):
        pl.when(group != me)(body)

    def loads_of(matrix):
        return (
            pltpu.make_async_copy(grads_hbm.at[matrix], grads.at[matrix], grads_sem.at[matrix]),
            pltpu.make_async_copy(
                momentum_hbm.at[matrix], momentum.at[matrix], momentum_sem.at[matrix]
            ),
        )

    def far_single(step):
        return (1 - upper) * inner + lax.rem(me + step, inner)

    def near_single(step):
        return upper * inner + lax.rem(me + step, inner)

    def double_at(step):
        return lax.rem(lax.rem(me, inner) + step, doubles)

    def fetch(matrix):
        for copy in loads_of(matrix):
            copy.start()

    owners_copy = pltpu.make_async_copy(owners_hbm, owners, owners_sem)
    barrier = pltpu.get_barrier_semaphore()

    @pl.loop(1, groups)
    def _(step):
        pl.semaphore_signal(barrier, inc=1, device_id=(group_at(step), part), device_id_type=MESH)

    for step in range(1, parts):
        peer = lax.rem(part + step, parts)
        pl.semaphore_signal(barrier, inc=1, device_id=(me, peer), device_id_type=MESH)

    @pl.loop(0, inner)
    def _(step):
        fetch(far_single(step))
        fetch(near_single(step))

    @pl.loop(0, doubles)
    def _(step):
        fetch(singles + double_at(step))

    owners_copy.start()

    def dir_copy(matrix, slot, which, group, source):
        return pltpu.make_async_remote_copy(
            src_ref=dirs.at[matrix], dst_ref=blocks.at[slot, source],
            send_sem=dir_send.at[matrix, which], recv_sem=dir_recv.at[slot, source],
            device_id=(group, part), device_id_type=MESH,
        )

    def direct(matrix):
        for copy in loads_of(matrix):
            copy.wait()
        grad_values = grads[matrix].astype(F32)
        new = muon_beta * momentum[matrix] + grad_values
        fresh[matrix] = new
        dirs[matrix] = (grad_values + muon_beta * new).astype(BF16)

    def send_single(matrix):
        owner = single_owner(matrix)
        elsewhere(owner, lambda: dir_copy(matrix, 0, 0, owner, me).start())

    def send_double(index, side):
        owner = double_owner(index, side)
        elsewhere(owner, lambda: dir_copy(singles + index, 1, side, owner, me).start())

    direct(far_single(0))
    pl.semaphore_wait(barrier, groups - 1 + parts - 1)
    send_single(far_single(0))
    direct(near_single(0))
    send_single(near_single(0))

    @pl.loop(1, inner)
    def _(step):
        direct(far_single(step))
        send_single(far_single(step))
        direct(near_single(step))
        send_single(near_single(step))

    @pl.loop(0, doubles)
    def _(step):
        index = double_at(step)
        direct(singles + index)
        send_double(index, 1 - upper)
        send_double(index, upper)

    mom_copy = pltpu.make_async_copy(fresh, momentum_new, mom_sem)
    mom_copy.start()

    def result_copy(slot, group, matrix):
        return pltpu.make_async_remote_copy(
            src_ref=results.at[slot, group], dst_ref=update.at[matrix],
            send_sem=res_send.at[slot, group], recv_sem=res_recv.at[matrix],
            device_id=(group, part), device_id_type=MESH,
        )

    def own_copy(slot, matrix):
        return pltpu.make_async_copy(results.at[slot, me], update.at[matrix], own_sem.at[slot])

    def load_copy(slot, group, place):
        return pltpu.make_async_remote_copy(
            src_ref=load_tile.at[slot], dst_ref=loads.at[place],
            send_sem=load_send.at[slot, group], recv_sem=load_recv.at[place],
            device_id=(group, part), device_id_type=MESH,
        )

    def peer_copy(buffer, slot, peer, place, send, recv):
        return pltpu.make_async_remote_copy(
            src_ref=buffer.at[slot, place], dst_ref=buffer.at[slot, place],
            send_sem=send.at[slot, peer], recv_sem=recv.at[slot, place],
            device_id=(me, peer), device_id_type=MESH,
        )

    per_chunk = groups // chunks
    chunk_rows = KV_OUT // chunks

    @pl.loop(0, 2)
    def _(slot):
        matrix = jnp.where(slot == 0, me - inner, singles + my_double)
        active = ((slot == 0) & has_single) | ((slot == 1) & has_double)
        place = jnp.where(slot == 0, matrix, matrix + upper * doubles)
        served = jnp.where(slot == 0, groups, half)

        @pl.when(active)
        def _():
            blocks[slot, me] = dirs[matrix]
            row_ids = lax.broadcasted_iota(jnp.int32, (KV_OUT, KV_OUT), 0)
            col_ids = lax.broadcasted_iota(jnp.int32, (KV_OUT, KV_OUT), 1)

            @pl.loop(1, groups)
            def _(step):
                dir_copy(matrix, slot, 0, me, group_at(step)).wait_recv()

            whole = blocks[slot].reshape(KV_OUT, cols)
            partial_value = lax.dot_general(
                whole, whole, (((1,), (1,)), ((), ())), preferred_element_type=F32
            )
            grams[slot, part] = partial_value.astype(BF16)
            squares = jnp.sum(jnp.where(row_ids == col_ids, partial_value, 0.0))
            traces[slot, part] = jnp.full((8, 128), squares, F32)
            for step in range(1, parts):
                peer = lax.rem(part + step, parts)
                peer_copy(grams, slot, peer, part, gram_send, gram_recv).start()
                peer_copy(traces, slot, peer, part, trace_send, trace_recv).start()
            for step in range(1, parts):
                peer = lax.rem(part + step, parts)
                peer_copy(grams, slot, peer, peer, gram_send, gram_recv).wait_recv()
                peer_copy(traces, slot, peer, peer, trace_send, trace_recv).wait_recv()
            gram_sum = jnp.sum(grams[slot].astype(F32), axis=0)
            square_sum = jnp.sum(traces[slot], axis=0)[0:1, 0:1]
            scale = 1.0 / (jnp.sqrt(square_sum) + norm_eps)
            gram = (gram_sum * scale * scale).astype(BF16)
            gram_wide = gram.astype(F32)
            poly = coef_b * gram_wide + coef_c * mul(gram, gram)
            poly_first = poly.astype(BF16)
            mixed = mul(poly_first, gram)
            next_gram = (
                (coef_a * coef_a) * gram_wide
                + (2.0 * coef_a) * mixed
                + mul(mixed.astype(BF16), poly_first)
            ).astype(BF16)
            poly_second = (
                coef_b * next_gram.astype(F32) + coef_c * mul(next_gram, next_gram)
            )
            total = (
                coef_a * (poly_first.astype(F32) + poly_second)
                + mul(poly_second.astype(BF16), poly_first)
            )
            ident[...] = total.astype(BF16).reshape(ident.shape)
            out_scale = scale * math.sqrt(D)

            def chunk_body(step, square_total):
                forward = jnp.where(slot == 0, upper == 1, upper == 0)
                chunk = jnp.where(forward, step, chunks - 1 - step)
                first = chunk * per_chunk
                mine = blocks[slot, pl.ds(first, per_chunk)].reshape(chunk_rows, cols)
                factor = ident[pl.ds(first, per_chunk)].reshape(chunk_rows, KV_OUT)
                values = (coef_a * coef_a) * mine.astype(F32) + mul(
                    factor, blocks[slot].reshape(KV_OUT, cols)
                )
                rounded = (out_scale * values).astype(BF16)
                results[slot, pl.ds(first, per_chunk)] = rounded.reshape(per_chunk, rows, cols)

                @pl.loop(0, per_chunk)
                def _(member):
                    group = first + lax.rem(me + member, per_chunk)
                    elsewhere(group, lambda: result_copy(slot, group, matrix).start())

                    @pl.when(group == me)
                    def _():
                        own_copy(slot, matrix).start()

                wide = rounded.astype(F32)
                return square_total + jnp.sum(wide * wide)

            square_total = lax.fori_loop(
                0, jnp.where(slot == 0, chunks, chunks // 2), chunk_body, jnp.zeros((), F32)
            )
            halves[slot, part] = jnp.full((8, 128), square_total, F32)
            for step in range(1, parts):
                peer = lax.rem(part + step, parts)
                peer_copy(halves, slot, peer, part, half_send, half_recv).start()
            for step in range(1, parts):
                peer = lax.rem(part + step, parts)
                peer_copy(halves, slot, peer, peer, half_send, half_recv).wait_recv()
            load_tile[slot] = jnp.sum(halves[slot], axis=0) / (KV_OUT * D)
            loads[place] = load_tile[slot]

            @pl.loop(1, groups)
            def _(step):
                load_copy(slot, group_at(step), place).start()

    @pl.loop(0, 2)
    def _(slot):
        matrix = jnp.where(slot == 0, me - inner, singles + my_double)
        active = ((slot == 0) & has_single) | ((slot == 1) & has_double)
        place = jnp.where(slot == 0, matrix, matrix + upper * doubles)
        first = jnp.where(slot == 0, 0, upper * half)
        served = jnp.where(slot == 0, groups, half)

        @pl.when(active)
        def _():
            for step in range(1, parts):
                peer = lax.rem(part + step, parts)
                peer_copy(grams, slot, peer, part, gram_send, gram_recv).wait_send()
                peer_copy(traces, slot, peer, part, trace_send, trace_recv).wait_send()
                peer_copy(halves, slot, peer, part, half_send, half_recv).wait_send()

            @pl.loop(0, served)
            def _(step):
                group = first + step
                elsewhere(group, lambda: result_copy(slot, group, matrix).wait_send())

            @pl.loop(1, groups)
            def _(step):
                load_copy(slot, group_at(step), place).wait_send()

            own_copy(slot, matrix).wait()

    @pl.loop(0, singles)
    def _(matrix):
        owner = single_owner(matrix)

        @pl.when(owner != me)
        def _():
            dir_copy(matrix, 0, 0, owner, me).wait_send()
            result_copy(0, me, matrix).wait_recv()
            load_copy(0, me, matrix).wait_recv()

    @pl.loop(0, doubles)
    def _(index):
        matrix = singles + index
        for side in range(2):
            owner = double_owner(index, side)

            @pl.when(owner != me)
            def _():
                dir_copy(matrix, 1, side, owner, me).wait_send()
                load_copy(1, me, matrix + side * doubles).wait_recv()

        elsewhere(
            double_owner(index, upper), lambda: result_copy(1, me, matrix).wait_recv()
        )

    owners_copy.wait()
    total_load = jnp.zeros((8, 128), F32)
    for matrix in range(mats):
        value = loads[matrix]
        if matrix >= singles:
            value = value + loads[matrix + doubles]
        total_load = total_load + jnp.where(owners[matrix] == me, 1.0, 0.0) * value
    owner_load[...] = total_load
    mom_copy.wait()


def finish(
    update, momentum, load_block, norm_grads, norm_params, adam_m, adam_v,
    update_out, momentum_out, load_out, params_out, adam_m_out, adam_v_out,
    update_sem, momentum_sem,
):
    momentum_copy = pltpu.make_async_copy(momentum, momentum_out, momentum_sem)
    update_copy = pltpu.make_async_copy(update, update_out, update_sem)
    momentum_copy.start()
    update_copy.start()
    grad = norm_grads[...]
    adam_m_new = adam_first * adam_m[...] + (1.0 - adam_first) * grad
    adam_v_new = adam_second * adam_v[...] + (1.0 - adam_second) * grad * grad
    corrected = adam_m_new / first_fix / (jnp.sqrt(adam_v_new / second_fix) + adam_eps)
    params_out[...] = norm_params[...] - adam_rate * corrected
    adam_m_out[...] = adam_m_new
    adam_v_out[...] = adam_v_new
    load_out[0] = load_block[0, 0]
    momentum_copy.wait()
    update_copy.wait()


def on_device(groups, parts, grads, momentum, owners, norm_grads, norm_params, adam_m, adam_v):
    mats, rows, cols = grads.shape
    places = mats + (mats - groups // 2)
    dma = pltpu.SemaphoreType.DMA
    vmem = pl.BlockSpec(memory_space=pltpu.VMEM)
    hbm = pl.BlockSpec(memory_space=pl.ANY)
    update, momentum_new, load_block = pl.pallas_call(
        functools.partial(kernel, groups, parts, mats, 4),
        out_shape=(
            jax.ShapeDtypeStruct((mats, rows, cols), BF16),
            jax.ShapeDtypeStruct((mats, rows, cols), F32),
            jax.ShapeDtypeStruct((8, 128), F32),
        ),
        in_specs=[pl.BlockSpec(memory_space=pltpu.HBM)] * 3,
        out_specs=(hbm, hbm, vmem),
        scratch_shapes=[
            pltpu.VMEM((mats, rows, cols), BF16),
            pltpu.VMEM((2, groups, rows, cols), BF16),
            pltpu.VMEM((2, groups, rows, cols), BF16),
            pltpu.VMEM((2, parts, KV_OUT, KV_OUT), BF16),
            pltpu.VMEM((2, parts, 8, 128), F32),
            pltpu.VMEM((2, parts, 8, 128), F32),
            pltpu.VMEM((2, 8, 128), F32),
            pltpu.VMEM((places, 8, 128), F32),
            pltpu.VMEM((mats, rows, cols), F32),
            pltpu.VMEM((groups, rows, KV_OUT), BF16),
            dma((mats, 2)), dma((2, groups)), dma((2, groups)), dma((mats,)),
            dma((2, parts)), dma((2, parts)), dma((2, parts)), dma((2, parts)),
            dma((2, parts)), dma((2, parts)), dma((2, groups)), dma((places,)),
            dma((2,)), dma,
            pltpu.SMEM((mats,), jnp.int32),
            pltpu.VMEM((mats, rows, cols), BF16),
            pltpu.VMEM((mats, rows, cols), F32),
            dma, dma((mats,)), dma((mats,)),
        ],
        compiler_params=pltpu.CompilerParams(
            collective_id=0, has_side_effects=True, vmem_limit_bytes=60 * 1024 * 1024
        ),
    )(owners, grads, momentum)
    norm_shape = jax.ShapeDtypeStruct(norm_grads.shape, F32)
    update, momentum_new, owner_load, norm_params_new, adam_m_new, adam_v_new = pl.pallas_call(
        finish,
        out_shape=(
            jax.ShapeDtypeStruct(update.shape, BF16),
            jax.ShapeDtypeStruct(momentum_new.shape, F32),
            jax.ShapeDtypeStruct((1,), F32),
            norm_shape, norm_shape, norm_shape,
        ),
        in_specs=[vmem] * 7,
        out_specs=(hbm, hbm, pl.BlockSpec(memory_space=pltpu.SMEM), vmem, vmem, vmem),
        scratch_shapes=[dma, dma],
    )(update, momentum_new, load_block, norm_grads, norm_params, adam_m, adam_v)
    return (update, momentum_new, owner_load, norm_params_new, adam_m_new, adam_v_new)


def solution(mesh):
    return jax.shard_map(
        functools.partial(on_device, mesh.shape["wide"], mesh.shape["narrow"]),
        mesh=mesh,
        in_specs=(
            P(None, "wide", "narrow"),
            P(None, "wide", "narrow"),
            P(),
            P("narrow", "wide"),
            P("narrow", "wide"),
            P("narrow", "wide"),
            P("narrow", "wide"),
        ),
        out_specs=(
            P(None, "wide", "narrow"),
            P(None, "wide", "narrow"),
            P("wide"),
            P("narrow", "wide"),
            P("narrow", "wide"),
            P("narrow", "wide"),
        ),
        check_vma=False,
    )
```

```python
import functools
import math

import jax
import jax.numpy as jnp
from jax import lax
from jax.experimental import pallas as pl
from jax.experimental.pallas import tpu as pltpu
from jax.sharding import PartitionSpec as P

D = 2048
KV_OUT = 512

coef_a = 3.4445
coef_b = -4.775
coef_c = 2.0315
muon_beta = 0.95
norm_eps = 1e-07
adam_first = 0.9
adam_second = 0.95
adam_rate = 0.02
adam_eps = 1e-08
first_fix = 1.0 - 0.9**10
second_fix = 1.0 - 0.95**10

MESH = pl.DeviceIdType.MESH
BF16 = jnp.bfloat16
F32 = jnp.float32


def mul(left, right):
    return jnp.dot(left, right, preferred_element_type=F32)


def kernel(
    groups, parts, mats, chunks,
    owners_hbm, grads_hbm, momentum_hbm,
    update, momentum_new, owner_load,
    dirs, blocks, results, grams, traces, halves, load_tile, loads, fresh, ident,
    dir_send, dir_recv, res_send, res_recv, gram_send, gram_recv,
    trace_send, trace_recv, half_send, half_recv, load_send, load_recv, own_sem, mom_sem,
    owners, grads, momentum, owners_sem, grads_sem, momentum_sem,
):
    me = lax.axis_index("wide")
    part = lax.axis_index("narrow")
    rows, cols = dirs.shape[1], dirs.shape[2]
    half = groups // 2
    inner = half // 2
    singles = half
    doubles = mats - singles
    upper = lax.div(me, half)

    def single_owner(matrix):
        return inner + matrix

    def double_owner(index, side):
        return jnp.where(side == 0, index, groups - 1 - index)

    my_double = jnp.where(upper == 0, me, groups - 1 - me)
    has_single = (me >= inner) & (me < inner + singles)
    has_double = my_double < doubles

    def group_at(step):
        return lax.rem(me + step, groups)

    def elsewhere(group, body):
        pl.when(group != me)(body)

    def loads_of(matrix):
        return (
            pltpu.make_async_copy(grads_hbm.at[matrix], grads.at[matrix], grads_sem.at[matrix]),
            pltpu.make_async_copy(
                momentum_hbm.at[matrix], momentum.at[matrix], momentum_sem.at[matrix]
            ),
        )

    def far_single(step):
        return (1 - upper) * inner + lax.rem(me + step, inner)

    def near_single(step):
        return upper * inner + lax.rem(me + step, inner)

    def double_at(step):
        return lax.rem(lax.rem(me, inner) + step, doubles)

    def fetch(matrix):
        for copy in loads_of(matrix):
            copy.start()

    owners_copy = pltpu.make_async_copy(owners_hbm, owners, owners_sem)
    barrier = pltpu.get_barrier_semaphore()

    @pl.loop(1, groups)
    def _(step):
        pl.semaphore_signal(barrier, inc=1, device_id=(group_at(step), part), device_id_type=MESH)

    for step in range(1, parts):
        peer = lax.rem(part + step, parts)
        pl.semaphore_signal(barrier, inc=1, device_id=(me, peer), device_id_type=MESH)

    @pl.loop(0, inner)
    def _(step):
        fetch(far_single(step))
        fetch(near_single(step))

    @pl.loop(0, doubles)
    def _(step):
        fetch(singles + double_at(step))

    owners_copy.start()

    def dir_copy(matrix, slot, which, group, source):
        return pltpu.make_async_remote_copy(
            src_ref=dirs.at[matrix], dst_ref=blocks.at[slot, source],
            send_sem=dir_send.at[matrix, which], recv_sem=dir_recv.at[slot, source],
            device_id=(group, part), device_id_type=MESH,
        )

    def direct(matrix):
        for copy in loads_of(matrix):
            copy.wait()
        grad_values = grads[matrix].astype(F32)
        new = muon_beta * momentum[matrix] + grad_values
        fresh[matrix] = new
        dirs[matrix] = (grad_values + muon_beta * new).astype(BF16)

    def send_single(matrix):
        owner = single_owner(matrix)
        elsewhere(owner, lambda: dir_copy(matrix, 0, 0, owner, me).start())

    def send_double(index, side):
        owner = double_owner(index, side)
        elsewhere(owner, lambda: dir_copy(singles + index, 1, side, owner, me).start())

    direct(far_single(0))
    pl.semaphore_wait(barrier, groups - 1 + parts - 1)
    send_single(far_single(0))
    direct(near_single(0))
    send_single(near_single(0))

    @pl.loop(1, inner)
    def _(step):
        direct(far_single(step))
        send_single(far_single(step))
        direct(near_single(step))
        send_single(near_single(step))

    @pl.loop(0, doubles)
    def _(step):
        index = double_at(step)
        direct(singles + index)
        send_double(index, 1 - upper)
        send_double(index, upper)

    mom_copy = pltpu.make_async_copy(fresh, momentum_new, mom_sem)
    mom_copy.start()

    def result_copy(slot, group, matrix):
        return pltpu.make_async_remote_copy(
            src_ref=results.at[slot, group], dst_ref=update.at[matrix],
            send_sem=res_send.at[slot, group], recv_sem=res_recv.at[matrix],
            device_id=(group, part), device_id_type=MESH,
        )

    def own_copy(slot, matrix):
        return pltpu.make_async_copy(results.at[slot, me], update.at[matrix], own_sem.at[slot])

    def load_copy(slot, group, place):
        return pltpu.make_async_remote_copy(
            src_ref=load_tile.at[slot], dst_ref=loads.at[place],
            send_sem=load_send.at[slot, group], recv_sem=load_recv.at[place],
            device_id=(group, part), device_id_type=MESH,
        )

    def peer_copy(buffer, slot, peer, place, send, recv):
        return pltpu.make_async_remote_copy(
            src_ref=buffer.at[slot, place], dst_ref=buffer.at[slot, place],
            send_sem=send.at[slot, peer], recv_sem=recv.at[slot, place],
            device_id=(me, peer), device_id_type=MESH,
        )

    per_chunk = groups // chunks
    chunk_rows = KV_OUT // chunks

    @pl.loop(0, 2)
    def _(slot):
        matrix = jnp.where(slot == 0, me - inner, singles + my_double)
        active = ((slot == 0) & has_single) | ((slot == 1) & has_double)
        place = jnp.where(slot == 0, matrix, matrix + upper * doubles)
        served = jnp.where(slot == 0, groups, half)

        @pl.when(active)
        def _():
            blocks[slot, me] = dirs[matrix]
            row_ids = lax.broadcasted_iota(jnp.int32, (KV_OUT, KV_OUT), 0)
            col_ids = lax.broadcasted_iota(jnp.int32, (KV_OUT, KV_OUT), 1)

            @pl.loop(1, groups)
            def _(step):
                dir_copy(matrix, slot, 0, me, group_at(step)).wait_recv()

            whole = blocks[slot].reshape(KV_OUT, cols)
            partial_value = lax.dot_general(
                whole, whole, (((1,), (1,)), ((), ())), preferred_element_type=F32
            )
            grams[slot, part] = partial_value.astype(BF16)
            squares = jnp.sum(jnp.where(row_ids == col_ids, partial_value, 0.0))
            traces[slot, part] = jnp.full((8, 128), squares, F32)
            for step in range(1, parts):
                peer = lax.rem(part + step, parts)
                peer_copy(grams, slot, peer, part, gram_send, gram_recv).start()
                peer_copy(traces, slot, peer, part, trace_send, trace_recv).start()
            for step in range(1, parts):
                peer = lax.rem(part + step, parts)
                peer_copy(grams, slot, peer, peer, gram_send, gram_recv).wait_recv()
                peer_copy(traces, slot, peer, peer, trace_send, trace_recv).wait_recv()
            gram_sum = jnp.sum(grams[slot].astype(F32), axis=0)
            square_sum = jnp.sum(traces[slot], axis=0)[0:1, 0:1]
            scale = 1.0 / (jnp.sqrt(square_sum) + norm_eps)
            gram = (gram_sum * scale * scale).astype(BF16)
            gram_wide = gram.astype(F32)
            poly = coef_b * gram_wide + coef_c * mul(gram, gram)
            poly_first = poly.astype(BF16)
            mixed = mul(poly_first, gram)
            next_gram = (
                (coef_a * coef_a) * gram_wide
                + (2.0 * coef_a) * mixed
                + mul(mixed.astype(BF16), poly_first)
            ).astype(BF16)
            poly_second = (
                coef_b * next_gram.astype(F32) + coef_c * mul(next_gram, next_gram)
            )
            total = (
                coef_a * (poly_first.astype(F32) + poly_second)
                + mul(poly_second.astype(BF16), poly_first)
            )
            ident[...] = total.astype(BF16).reshape(ident.shape)
            out_scale = scale * math.sqrt(D)

            def chunk_body(step, square_total):
                forward = jnp.where(slot == 0, upper == 1, upper == 0)
                chunk = jnp.where(forward, step, chunks - 1 - step)
                first = chunk * per_chunk
                mine = blocks[slot, pl.ds(first, per_chunk)].reshape(chunk_rows, cols)
                factor = ident[pl.ds(first, per_chunk)].reshape(chunk_rows, KV_OUT)
                values = (coef_a * coef_a) * mine.astype(F32) + mul(
                    factor, blocks[slot].reshape(KV_OUT, cols)
                )
                rounded = (out_scale * values).astype(BF16)
                results[slot, pl.ds(first, per_chunk)] = rounded.reshape(per_chunk, rows, cols)

                @pl.loop(0, per_chunk)
                def _(member):
                    group = first + lax.rem(me + member, per_chunk)
                    elsewhere(group, lambda: result_copy(slot, group, matrix).start())

                    @pl.when(group == me)
                    def _():
                        own_copy(slot, matrix).start()

                wide = rounded.astype(F32)
                return square_total + jnp.sum(wide * wide)

            square_total = lax.fori_loop(
                0, jnp.where(slot == 0, chunks, chunks // 2), chunk_body, jnp.zeros((), F32)
            )
            halves[slot, part] = jnp.full((8, 128), square_total, F32)
            for step in range(1, parts):
                peer = lax.rem(part + step, parts)
                peer_copy(halves, slot, peer, part, half_send, half_recv).start()
            for step in range(1, parts):
                peer = lax.rem(part + step, parts)
                peer_copy(halves, slot, peer, peer, half_send, half_recv).wait_recv()
            load_tile[slot] = jnp.sum(halves[slot], axis=0) / (KV_OUT * D)
            loads[place] = load_tile[slot]

            @pl.loop(1, groups)
            def _(step):
                load_copy(slot, group_at(step), place).start()

    @pl.loop(0, 2)
    def _(slot):
        matrix = jnp.where(slot == 0, me - inner, singles + my_double)
        active = ((slot == 0) & has_single) | ((slot == 1) & has_double)
        place = jnp.where(slot == 0, matrix, matrix + upper * doubles)
        first = jnp.where(slot == 0, 0, upper * half)
        served = jnp.where(slot == 0, groups, half)

        @pl.when(active)
        def _():
            for step in range(1, parts):
                peer = lax.rem(part + step, parts)
                peer_copy(grams, slot, peer, part, gram_send, gram_recv).wait_send()
                peer_copy(traces, slot, peer, part, trace_send, trace_recv).wait_send()
                peer_copy(halves, slot, peer, part, half_send, half_recv).wait_send()

            @pl.loop(0, served)
            def _(step):
                group = first + step
                elsewhere(group, lambda: result_copy(slot, group, matrix).wait_send())

            @pl.loop(1, groups)
            def _(step):
                load_copy(slot, group_at(step), place).wait_send()

            own_copy(slot, matrix).wait()

    @pl.loop(0, singles)
    def _(matrix):
        owner = single_owner(matrix)

        @pl.when(owner != me)
        def _():
            dir_copy(matrix, 0, 0, owner, me).wait_send()
            result_copy(0, me, matrix).wait_recv()
            load_copy(0, me, matrix).wait_recv()

    @pl.loop(0, doubles)
    def _(index):
        matrix = singles + index
        for side in range(2):
            owner = double_owner(index, side)

            @pl.when(owner != me)
            def _():
                dir_copy(matrix, 1, side, owner, me).wait_send()
                load_copy(1, me, matrix + side * doubles).wait_recv()

        elsewhere(
            double_owner(index, upper), lambda: result_copy(1, me, matrix).wait_recv()
        )

    owners_copy.wait()
    total_load = jnp.zeros((8, 128), F32)
    for matrix in range(mats):
        value = loads[matrix]
        if matrix >= singles:
            value = value + loads[matrix + doubles]
        total_load = total_load + jnp.where(owners[matrix] == me, 1.0, 0.0) * value
    owner_load[...] = total_load
    mom_copy.wait()


def finish(
    update, momentum, load_block, norm_grads, norm_params, adam_m, adam_v,
    update_out, momentum_out, load_out, params_out, adam_m_out, adam_v_out,
    update_sem, momentum_sem,
):
    momentum_copy = pltpu.make_async_copy(momentum, momentum_out, momentum_sem)
    update_copy = pltpu.make_async_copy(update, update_out, update_sem)
    momentum_copy.start()
    update_copy.start()
    grad = norm_grads[...]
    adam_m_new = adam_first * adam_m[...] + (1.0 - adam_first) * grad
    adam_v_new = adam_second * adam_v[...] + (1.0 - adam_second) * grad * grad
    corrected = adam_m_new / first_fix / (jnp.sqrt(adam_v_new / second_fix) + adam_eps)
    params_out[...] = norm_params[...] - adam_rate * corrected
    adam_m_out[...] = adam_m_new
    adam_v_out[...] = adam_v_new
    load_out[0] = load_block[0, 0]
    momentum_copy.wait()
    update_copy.wait()


def on_device(groups, parts, grads, momentum, owners, norm_grads, norm_params, adam_m, adam_v):
    mats, rows, cols = grads.shape
    places = mats + (mats - groups // 2)
    dma = pltpu.SemaphoreType.DMA
    vmem = pl.BlockSpec(memory_space=pltpu.VMEM)
    hbm = pl.BlockSpec(memory_space=pl.ANY)
    update, momentum_new, load_block = pl.pallas_call(
        functools.partial(kernel, groups, parts, mats, 4),
        out_shape=(
            jax.ShapeDtypeStruct((mats, rows, cols), BF16),
            jax.ShapeDtypeStruct((mats, rows, cols), F32),
            jax.ShapeDtypeStruct((8, 128), F32),
        ),
        in_specs=[pl.BlockSpec(memory_space=pltpu.HBM)] * 3,
        out_specs=(hbm, hbm, vmem),
        scratch_shapes=[
            pltpu.VMEM((mats, rows, cols), BF16),
            pltpu.VMEM((2, groups, rows, cols), BF16),
            pltpu.VMEM((2, groups, rows, cols), BF16),
            pltpu.VMEM((2, parts, KV_OUT, KV_OUT), BF16),
            pltpu.VMEM((2, parts, 8, 128), F32),
            pltpu.VMEM((2, parts, 8, 128), F32),
            pltpu.VMEM((2, 8, 128), F32),
            pltpu.VMEM((places, 8, 128), F32),
            pltpu.VMEM((mats, rows, cols), F32),
            pltpu.VMEM((groups, rows, KV_OUT), BF16),
            dma((mats, 2)), dma((2, groups)), dma((2, groups)), dma((mats,)),
            dma((2, parts)), dma((2, parts)), dma((2, parts)), dma((2, parts)),
            dma((2, parts)), dma((2, parts)), dma((2, groups)), dma((places,)),
            dma((2,)), dma,
            pltpu.SMEM((mats,), jnp.int32),
            pltpu.VMEM((mats, rows, cols), BF16),
            pltpu.VMEM((mats, rows, cols), F32),
            dma, dma((mats,)), dma((mats,)),
        ],
        compiler_params=pltpu.CompilerParams(
            collective_id=0, has_side_effects=True, vmem_limit_bytes=28 * 1024 * 1024
        ),
    )(*(pltpu.with_memory_space_constraint(array, pltpu.HBM) for array in (owners, grads, momentum)))
    norm_shape = jax.ShapeDtypeStruct(norm_grads.shape, F32)
    update, momentum_new, owner_load, norm_params_new, adam_m_new, adam_v_new = pl.pallas_call(
        finish,
        out_shape=(
            jax.ShapeDtypeStruct(update.shape, BF16),
            jax.ShapeDtypeStruct(momentum_new.shape, F32),
            jax.ShapeDtypeStruct((1,), F32),
            norm_shape, norm_shape, norm_shape,
        ),
        in_specs=[hbm, hbm] + [vmem] * 5,
        out_specs=(
            pl.BlockSpec(memory_space=pltpu.HBM), pl.BlockSpec(memory_space=pltpu.HBM),
            pl.BlockSpec(memory_space=pltpu.SMEM), vmem, vmem, vmem,
        ),
        scratch_shapes=[dma, dma],
        compiler_params=pltpu.CompilerParams(vmem_limit_bytes=8 * 1024 * 1024),
    )(update, momentum_new, load_block, norm_grads, norm_params, adam_m, adam_v)
    return (update, momentum_new, owner_load, norm_params_new, adam_m_new, adam_v_new)


def solution(mesh):
    return jax.shard_map(
        functools.partial(on_device, mesh.shape["wide"], mesh.shape["narrow"]),
        mesh=mesh,
        in_specs=(
            P(None, "wide", "narrow"),
            P(None, "wide", "narrow"),
            P(),
            P("narrow", "wide"),
            P("narrow", "wide"),
            P("narrow", "wide"),
            P("narrow", "wide"),
        ),
        out_specs=(
            P(None, "wide", "narrow"),
            P(None, "wide", "narrow"),
            P("wide"),
            P("narrow", "wide"),
            P("narrow", "wide"),
            P("narrow", "wide"),
        ),
        check_vma=False,
    )
```

```python
import functools
import math

import jax
import jax.numpy as jnp
from jax import lax
from jax.experimental import pallas as pl
from jax.experimental.pallas import tpu as pltpu
from jax.sharding import PartitionSpec as P

D = 2048
KV_OUT = 512

coef_a = 3.4445
coef_b = -4.775
coef_c = 2.0315
muon_beta = 0.95
norm_eps = 1e-07
adam_first = 0.9
adam_second = 0.95
adam_rate = 0.02
adam_eps = 1e-08
first_fix = 1.0 - 0.9**10
second_fix = 1.0 - 0.95**10

MESH = pl.DeviceIdType.MESH
BF16 = jnp.bfloat16
F32 = jnp.float32


def mul(left, right):
    return jnp.dot(left, right, preferred_element_type=F32)


def kernel(
    groups, parts, mats, chunks,
    owners_hbm, grads_hbm, momentum_hbm,
    update, momentum_new, owner_load,
    dirs, blocks, results, grams, traces, halves, load_tile, loads, fresh, ident,
    dir_send, dir_recv, res_send, res_recv, gram_send, gram_recv,
    trace_send, trace_recv, half_send, half_recv, load_send, load_recv, own_sem, mom_sem, turn,
    owners, grads, momentum, owners_sem, grads_sem, momentum_sem,
):
    me = lax.axis_index("wide")
    part = lax.axis_index("narrow")
    rows, cols = dirs.shape[1], dirs.shape[2]
    half = groups // 2
    inner = half // 2
    singles = half
    doubles = mats - singles
    upper = lax.div(me, half)

    def single_owner(matrix):
        return inner + matrix

    def double_owner(index, side):
        return jnp.where(side == 0, index, groups - 1 - index)

    my_double = jnp.where(upper == 0, me, groups - 1 - me)
    has_single = (me >= inner) & (me < inner + singles)
    has_double = my_double < doubles

    def group_at(step):
        return lax.rem(me + step, groups)

    def elsewhere(group, body):
        pl.when(group != me)(body)

    def loads_of(matrix):
        return (
            pltpu.make_async_copy(grads_hbm.at[matrix], grads.at[matrix], grads_sem.at[matrix]),
            pltpu.make_async_copy(
                momentum_hbm.at[matrix], momentum.at[matrix], momentum_sem.at[matrix]
            ),
        )

    def far_single(step):
        return (1 - upper) * inner + lax.rem(me + step, inner)

    def near_single(step):
        return upper * inner + lax.rem(me + step, inner)

    def double_at(step):
        return lax.rem(lax.rem(me, inner) + step, doubles)

    def fetch(matrix):
        for copy in loads_of(matrix):
            copy.start()

    owners_copy = pltpu.make_async_copy(owners_hbm, owners, owners_sem)
    barrier = pltpu.get_barrier_semaphore()

    @pl.loop(1, groups)
    def _(step):
        pl.semaphore_signal(barrier, inc=1, device_id=(group_at(step), part), device_id_type=MESH)

    for step in range(1, parts):
        peer = lax.rem(part + step, parts)
        pl.semaphore_signal(barrier, inc=1, device_id=(me, peer), device_id_type=MESH)

    @pl.loop(0, inner)
    def _(step):
        fetch(far_single(step))
        fetch(near_single(step))

    @pl.loop(0, doubles)
    def _(step):
        fetch(singles + double_at(step))


    owners_copy.start()

    def dir_copy(matrix, slot, which, group, source):
        return pltpu.make_async_remote_copy(
            src_ref=dirs.at[matrix], dst_ref=blocks.at[slot, source],
            send_sem=dir_send.at[matrix, which], recv_sem=dir_recv.at[slot, source],
            device_id=(group, part), device_id_type=MESH,
        )

    def direct(matrix):
        for copy in loads_of(matrix):
            copy.wait()
        grad_values = grads[matrix].astype(F32)
        new = muon_beta * momentum[matrix] + grad_values
        fresh[matrix] = new
        dirs[matrix] = (grad_values + muon_beta * new).astype(BF16)

    def send_single(matrix):
        owner = single_owner(matrix)
        elsewhere(owner, lambda: dir_copy(matrix, 0, 0, owner, me).start())

    def send_double(index, side):
        owner = double_owner(index, side)
        elsewhere(owner, lambda: dir_copy(singles + index, 1, side, owner, me).start())

    def pass_single(matrix):
        direct(matrix)
        send_single(matrix)

    def pass_double(index):
        direct(singles + index)
        pl.when(jnp.logical_not(((me >= inner) & (me < groups - inner)) & (part > 0)))(lambda: send_double(index, 1 - upper))
        send_double(index, upper)

    pl.semaphore_wait(barrier, groups - 1 + parts - 1)

    @pl.loop(0, inner)
    def _(step):
        pass_single(far_single(step))
        pass_single(near_single(step))

    @pl.loop(0, doubles)
    def _(step):
        pass_double(double_at(step))

    def single_sent(step):
        matrix = far_single(step)
        dir_copy(matrix, 0, 0, single_owner(matrix), me).wait_send()

    @pl.when((me >= inner) & (me < groups - inner))
    def _():
        @pl.when(part == 0)
        def _():
            @pl.loop(0, inner)
            def _(step):
                single_sent(step)

            for peer in range(1, parts):
                pl.semaphore_signal(turn, inc=1, device_id=(me, peer), device_id_type=MESH)

        @pl.when(part > 0)
        def _():
            pl.semaphore_wait(turn, 1)

            @pl.loop(0, doubles)
            def _(step):
                send_double(double_at(step), 1 - upper)

    mom_copy = pltpu.make_async_copy(fresh, momentum_new, mom_sem)
    mom_copy.start()

    def result_copy(slot, group, matrix):
        return pltpu.make_async_remote_copy(
            src_ref=results.at[slot, group], dst_ref=update.at[matrix],
            send_sem=res_send.at[slot, group], recv_sem=res_recv.at[matrix],
            device_id=(group, part), device_id_type=MESH,
        )

    def own_copy(slot, matrix):
        return pltpu.make_async_copy(results.at[slot, me], update.at[matrix], own_sem.at[slot])

    def load_copy(slot, group, place):
        return pltpu.make_async_remote_copy(
            src_ref=load_tile.at[slot], dst_ref=loads.at[place],
            send_sem=load_send.at[slot, group], recv_sem=load_recv.at[place],
            device_id=(group, part), device_id_type=MESH,
        )

    def peer_copy(buffer, slot, peer, place, send, recv):
        return pltpu.make_async_remote_copy(
            src_ref=buffer.at[slot, place], dst_ref=buffer.at[slot, place],
            send_sem=send.at[slot, peer], recv_sem=recv.at[slot, place],
            device_id=(me, peer), device_id_type=MESH,
        )

    per_chunk = groups // chunks
    chunk_rows = KV_OUT // chunks

    @pl.loop(0, 2)
    def _(slot):
        matrix = jnp.where(slot == 0, me - inner, singles + my_double)
        active = ((slot == 0) & has_single) | ((slot == 1) & has_double)
        place = jnp.where(slot == 0, matrix, matrix + upper * doubles)
        served = jnp.where(slot == 0, groups, half)

        @pl.when(active)
        def _():
            blocks[slot, me] = dirs[matrix]
            row_ids = lax.broadcasted_iota(jnp.int32, (KV_OUT, KV_OUT), 0)
            col_ids = lax.broadcasted_iota(jnp.int32, (KV_OUT, KV_OUT), 1)

            @pl.loop(1, groups)
            def _(step):
                dir_copy(matrix, slot, 0, me, group_at(step)).wait_recv()

            whole = blocks[slot].reshape(KV_OUT, cols)
            partial_value = lax.dot_general(
                whole, whole, (((1,), (1,)), ((), ())), preferred_element_type=F32
            )
            grams[slot, part] = partial_value.astype(BF16)
            squares = jnp.sum(jnp.where(row_ids == col_ids, partial_value, 0.0))
            traces[slot, part] = jnp.full((8, 128), squares, F32)
            for step in range(1, parts):
                peer = lax.rem(part + step, parts)
                peer_copy(grams, slot, peer, part, gram_send, gram_recv).start()
                peer_copy(traces, slot, peer, part, trace_send, trace_recv).start()
            for step in range(1, parts):
                peer = lax.rem(part + step, parts)
                peer_copy(grams, slot, peer, peer, gram_send, gram_recv).wait_recv()
                peer_copy(traces, slot, peer, peer, trace_send, trace_recv).wait_recv()
            gram_sum = jnp.sum(grams[slot].astype(F32), axis=0)
            square_sum = jnp.sum(traces[slot], axis=0)[0:1, 0:1]
            scale = 1.0 / (jnp.sqrt(square_sum) + norm_eps)
            gram = (gram_sum * scale * scale).astype(BF16)
            gram_wide = gram.astype(F32)
            poly = coef_b * gram_wide + coef_c * mul(gram, gram)
            poly_first = poly.astype(BF16)
            mixed = mul(poly_first, gram)
            next_gram = (
                (coef_a * coef_a) * gram_wide
                + (2.0 * coef_a) * mixed
                + mul(mixed.astype(BF16), poly_first)
            ).astype(BF16)
            poly_second = (
                coef_b * next_gram.astype(F32) + coef_c * mul(next_gram, next_gram)
            )
            total = (
                coef_a * (poly_first.astype(F32) + poly_second)
                + mul(poly_second.astype(BF16), poly_first)
            )
            ident[...] = total.astype(BF16).reshape(ident.shape)
            out_scale = scale * math.sqrt(D)

            def chunk_at(step):
                forward = jnp.where(slot == 0, upper == 1, upper == 0)
                return jnp.where(forward, step, chunks - 1 - step)

            def send_chunk(first, start, stop):
                @pl.loop(start, stop)
                def _(member):
                    group = first + lax.rem(me + member, per_chunk)
                    elsewhere(group, lambda: result_copy(slot, group, matrix).start())

                    @pl.when(group == me)
                    def _():
                        own_copy(slot, matrix).start()

            def chunk_body(step, square_total):
                first = chunk_at(step) * per_chunk
                mine = blocks[slot, pl.ds(first, per_chunk)].reshape(chunk_rows, cols)
                factor = ident[pl.ds(first, per_chunk)].reshape(chunk_rows, KV_OUT)
                values = (coef_a * coef_a) * mine.astype(F32) + mul(
                    factor, blocks[slot].reshape(KV_OUT, cols)
                )
                rounded = (out_scale * values).astype(BF16)
                results[slot, pl.ds(first, per_chunk)] = rounded.reshape(per_chunk, rows, cols)

                wide = rounded.astype(F32)
                squares = jnp.sum((wide * wide).reshape(chunk_rows // 8, 8, cols), axis=0)
                for lane in range(0, cols, 128):
                    square_total = square_total + squares[:, lane : lane + 128]

                @pl.when(step == last)
                def _():
                    load_tile[slot] = square_total
                    loads[place] = square_total

                    @pl.loop(1, groups)
                    def _(step):
                        load_copy(slot, group_at(step), place).start()

                    send_chunk(chunk_at(step - 1) * per_chunk, 0, per_chunk)

                send_chunk(first, 0, jnp.where(step == last - 1, 0, per_chunk))
                return square_total

            last = jnp.where(slot == 0, chunks, chunks // 2) - 1
            lax.fori_loop(0, last + 1, chunk_body, jnp.zeros((8, 128), F32))

    @pl.loop(0, singles)
    def _(matrix):
        elsewhere(single_owner(matrix), lambda: load_copy(0, me, matrix).wait_recv())

    @pl.loop(0, doubles)
    def _(index):
        for side in range(2):
            elsewhere(
                double_owner(index, side),
                lambda: load_copy(1, me, singles + index + side * doubles).wait_recv(),
            )

    owners_copy.wait()
    total_load = jnp.zeros((8, 128), F32)
    for matrix in range(mats):
        value = loads[matrix]
        if matrix >= singles:
            value = value + loads[matrix + doubles]
        total_load = total_load + jnp.where(owners[matrix] == me, 1.0, 0.0) * value
    halves[part] = jnp.full((8, 128), jnp.sum(total_load), F32)

    def half_copy(peer, place):
        return pltpu.make_async_remote_copy(
            src_ref=halves.at[place], dst_ref=halves.at[place],
            send_sem=half_send.at[peer], recv_sem=half_recv.at[place],
            device_id=(me, peer), device_id_type=MESH,
        )

    for step in range(1, parts):
        half_copy(lax.rem(part + step, parts), part).start()

    @pl.loop(0, 2)
    def _(slot):
        matrix = jnp.where(slot == 0, me - inner, singles + my_double)
        active = ((slot == 0) & has_single) | ((slot == 1) & has_double)
        place = jnp.where(slot == 0, matrix, matrix + upper * doubles)
        first = jnp.where(slot == 0, 0, upper * half)
        served = jnp.where(slot == 0, groups, half)

        @pl.when(active)
        def _():
            for step in range(1, parts):
                peer = lax.rem(part + step, parts)
                peer_copy(grams, slot, peer, part, gram_send, gram_recv).wait_send()
                peer_copy(traces, slot, peer, part, trace_send, trace_recv).wait_send()

            @pl.loop(0, served)
            def _(step):
                group = first + step
                elsewhere(group, lambda: result_copy(slot, group, matrix).wait_send())

            @pl.loop(1, groups)
            def _(step):
                load_copy(slot, group_at(step), place).wait_send()

            own_copy(slot, matrix).wait()

    @pl.loop(0, singles)
    def _(matrix):
        owner = single_owner(matrix)

        @pl.when(owner != me)
        def _():
            waited = ((me >= inner) & (me < groups - inner)) & (part == 0) & (lax.div(matrix, inner) != upper)
            waited = waited & (lax.rem(matrix - lax.rem(me, inner) + inner, inner) < inner)
            pl.when(jnp.logical_not(waited))(lambda: dir_copy(matrix, 0, 0, owner, me).wait_send())
            result_copy(0, me, matrix).wait_recv()

    @pl.loop(0, doubles)
    def _(index):
        matrix = singles + index
        for side in range(2):
            owner = double_owner(index, side)

            @pl.when(owner != me)
            def _():
                dir_copy(matrix, 1, side, owner, me).wait_send()

        elsewhere(
            double_owner(index, upper), lambda: result_copy(1, me, matrix).wait_recv()
        )

    for step in range(1, parts):
        peer = lax.rem(part + step, parts)
        half_copy(peer, part).wait_send()
        half_copy(peer, peer).wait_recv()
    owner_load[...] = jnp.sum(halves[...], axis=0) / (KV_OUT * D)
    mom_copy.wait()


def finish(
    update, momentum, load_block, norm_grads, norm_params, adam_m, adam_v,
    update_out, momentum_out, load_out, params_out, adam_m_out, adam_v_out,
    update_sem, momentum_sem,
):
    momentum_copy = pltpu.make_async_copy(momentum, momentum_out, momentum_sem)
    update_copy = pltpu.make_async_copy(update, update_out, update_sem)
    momentum_copy.start()
    update_copy.start()
    grad = norm_grads[...]
    adam_m_new = adam_first * adam_m[...] + (1.0 - adam_first) * grad
    adam_v_new = adam_second * adam_v[...] + (1.0 - adam_second) * grad * grad
    corrected = adam_m_new / first_fix / (jnp.sqrt(adam_v_new / second_fix) + adam_eps)
    params_out[...] = norm_params[...] - adam_rate * corrected
    adam_m_out[...] = adam_m_new
    adam_v_out[...] = adam_v_new
    load_out[0] = load_block[0, 0]
    momentum_copy.wait()
    update_copy.wait()


def on_device(groups, parts, grads, momentum, owners, norm_grads, norm_params, adam_m, adam_v):
    mats, rows, cols = grads.shape
    places = mats + (mats - groups // 2)
    dma = pltpu.SemaphoreType.DMA
    vmem = pl.BlockSpec(memory_space=pltpu.VMEM)
    hbm = pl.BlockSpec(memory_space=pl.ANY)
    update, momentum_new, load_block = pl.pallas_call(
        functools.partial(kernel, groups, parts, mats, 4),
        out_shape=(
            jax.ShapeDtypeStruct((mats, rows, cols), BF16),
            jax.ShapeDtypeStruct((mats, rows, cols), F32),
            jax.ShapeDtypeStruct((8, 128), F32),
        ),
        in_specs=[pl.BlockSpec(memory_space=pltpu.HBM)] * 3,
        out_specs=(hbm, hbm, vmem),
        scratch_shapes=[
            pltpu.VMEM((mats, rows, cols), BF16),
            pltpu.VMEM((2, groups, rows, cols), BF16),
            pltpu.VMEM((2, groups, rows, cols), BF16),
            pltpu.VMEM((2, parts, KV_OUT, KV_OUT), BF16),
            pltpu.VMEM((2, parts, 8, 128), F32),
            pltpu.VMEM((parts, 8, 128), F32),
            pltpu.VMEM((2, 8, 128), F32),
            pltpu.VMEM((places, 8, 128), F32),
            pltpu.VMEM((mats, rows, cols), F32),
            pltpu.VMEM((groups, rows, KV_OUT), BF16),
            dma((mats, 2)), dma((2, groups)), dma((2, groups)), dma((mats,)),
            dma((2, parts)), dma((2, parts)), dma((2, parts)), dma((2, parts)),
            dma((parts,)), dma((parts,)), dma((2, groups)), dma((places,)),
            dma((2,)), dma, pltpu.SemaphoreType.REGULAR,
            pltpu.SMEM((mats,), jnp.int32),
            pltpu.VMEM((mats, rows, cols), BF16),
            pltpu.VMEM((mats, rows, cols), F32),
            dma, dma((mats,)), dma((mats,)),
        ],
        compiler_params=pltpu.CompilerParams(
            collective_id=0, has_side_effects=True, vmem_limit_bytes=28 * 1024 * 1024
        ),
    )(*(pltpu.with_memory_space_constraint(array, pltpu.HBM) for array in (owners, grads, momentum)))
    norm_shape = jax.ShapeDtypeStruct(norm_grads.shape, F32)
    update, momentum_new, owner_load, norm_params_new, adam_m_new, adam_v_new = pl.pallas_call(
        finish,
        out_shape=(
            jax.ShapeDtypeStruct(update.shape, BF16),
            jax.ShapeDtypeStruct(momentum_new.shape, F32),
            jax.ShapeDtypeStruct((1,), F32),
            norm_shape, norm_shape, norm_shape,
        ),
        in_specs=[hbm, hbm] + [vmem] * 5,
        out_specs=(
            pl.BlockSpec(memory_space=pltpu.HBM), pl.BlockSpec(memory_space=pltpu.HBM),
            pl.BlockSpec(memory_space=pltpu.SMEM), vmem, vmem, vmem,
        ),
        scratch_shapes=[dma, dma],
        compiler_params=pltpu.CompilerParams(vmem_limit_bytes=8 * 1024 * 1024),
    )(update, momentum_new, load_block, norm_grads, norm_params, adam_m, adam_v)
    return (update, momentum_new, owner_load, norm_params_new, adam_m_new, adam_v_new)


def solution(mesh):
    return jax.shard_map(
        functools.partial(on_device, mesh.shape["wide"], mesh.shape["narrow"]),
        mesh=mesh,
        in_specs=(
            P(None, "wide", "narrow"),
            P(None, "wide", "narrow"),
            P(),
            P("narrow", "wide"),
            P("narrow", "wide"),
            P("narrow", "wide"),
            P("narrow", "wide"),
        ),
        out_specs=(
            P(None, "wide", "narrow"),
            P(None, "wide", "narrow"),
            P("wide"),
            P("narrow", "wide"),
            P("narrow", "wide"),
            P("narrow", "wide"),
        ),
        check_vma=False,
    )
```

```python
import functools
import math

import jax
import jax.numpy as jnp
from jax import lax
from jax.experimental import pallas as pl
from jax.experimental.pallas import tpu as pltpu
from jax.sharding import PartitionSpec as P

D = 2048
KV_OUT = 512

coef_a = 3.4445
coef_b = -4.775
coef_c = 2.0315
muon_beta = 0.95
norm_eps = 1e-07
adam_first = 0.9
adam_second = 0.95
adam_rate = 0.02
adam_eps = 1e-08
first_fix = 1.0 - 0.9**10
second_fix = 1.0 - 0.95**10

MESH = pl.DeviceIdType.MESH
BF16 = jnp.bfloat16
F32 = jnp.float32


def mul(left, right):
    return jnp.dot(left, right, preferred_element_type=F32)


def kernel(
    groups, parts, mats, chunks,
    owners_hbm, grads_hbm, momentum_hbm,
    update, momentum_new, owner_load,
    dirs, blocks, results, grams, traces, halves, load_tile, loads, fresh, ident,
    dir_send, dir_recv, res_send, res_recv, gram_send, gram_recv,
    trace_send, trace_recv, half_send, half_recv, load_send, load_recv, own_sem, mom_sem, turn, ready,
    owners, grads, momentum, owners_sem, grads_sem, momentum_sem,
):
    me = lax.axis_index("wide")
    part = lax.axis_index("narrow")
    rows, cols = dirs.shape[1], dirs.shape[2]
    half = groups // 2
    inner = half // 2
    singles = half
    doubles = mats - singles
    upper = lax.div(me, half)

    def single_owner(matrix):
        return inner + matrix

    def double_owner(index, side):
        return jnp.where(side == 0, index, groups - 1 - index)

    my_double = jnp.where(upper == 0, me, groups - 1 - me)
    has_single = (me >= inner) & (me < inner + singles)
    has_double = my_double < doubles

    def group_at(step):
        return lax.rem(me + step, groups)

    def elsewhere(group, body):
        pl.when(group != me)(body)

    def loads_of(matrix):
        return (
            pltpu.make_async_copy(grads_hbm.at[matrix], grads.at[matrix], grads_sem.at[matrix]),
            pltpu.make_async_copy(
                momentum_hbm.at[matrix], momentum.at[matrix], momentum_sem.at[matrix]
            ),
        )

    def far_single(step):
        return (1 - upper) * inner + lax.rem(me + step, inner)

    def near_single(step):
        return upper * inner + lax.rem(me + step, inner)

    def double_at(step):
        return lax.rem(lax.rem(me, inner) + step, doubles)

    def fetch(matrix):
        for copy in loads_of(matrix):
            copy.start()

    owners_copy = pltpu.make_async_copy(owners_hbm, owners, owners_sem)
    barrier = pltpu.get_barrier_semaphore()
    outer = (me < inner) | (me >= groups - inner)

    def inner_at(step):
        return inner + lax.rem(lax.rem(me + inner, half) + step, half)

    @pl.loop(1, groups)
    def _(step):
        group = group_at(step)
        group_outer = (group < inner) | (group >= groups - inner)

        @pl.when(group_outer | jnp.logical_not(outer))
        def _():
            pl.semaphore_signal(barrier, inc=1, device_id=(group, part), device_id_type=MESH)

    for step in range(1, parts):
        peer = lax.rem(part + step, parts)
        pl.semaphore_signal(barrier, inc=1, device_id=(me, peer), device_id_type=MESH)

    @pl.loop(0, inner)
    def _(step):
        fetch(far_single(step))
        fetch(near_single(step))

    @pl.loop(0, doubles)
    def _(step):
        fetch(singles + double_at(step))


    owners_copy.start()

    def dir_copy(matrix, slot, which, group, source):
        return pltpu.make_async_remote_copy(
            src_ref=dirs.at[matrix], dst_ref=blocks.at[slot, source],
            send_sem=dir_send.at[matrix, which], recv_sem=dir_recv.at[slot, source],
            device_id=(group, part), device_id_type=MESH,
        )

    def direct(matrix):
        for copy in loads_of(matrix):
            copy.wait()
        grad_values = grads[matrix].astype(F32)
        new = muon_beta * momentum[matrix] + grad_values
        fresh[matrix] = new
        dirs[matrix] = (grad_values + muon_beta * new).astype(BF16)

    def send_single(matrix):
        owner = single_owner(matrix)
        elsewhere(owner, lambda: dir_copy(matrix, 0, 0, owner, me).start())

    def send_double(index, side):
        owner = double_owner(index, side)
        elsewhere(owner, lambda: dir_copy(singles + index, 1, side, owner, me).start())

    def pass_single(matrix):
        direct(matrix)
        send_single(matrix)

    def pass_double(index):
        direct(singles + index)
        pl.when(jnp.logical_not(((me >= inner) & (me < groups - inner)) & (part > 0)))(lambda: send_double(index, 1 - upper))
        send_double(index, upper)

    @pl.when(outer)
    def _():
        pl.semaphore_wait(barrier, groups - 1 + parts - 1)

        @pl.loop(0, half)
        def _(step):
            pl.semaphore_signal(
                ready, inc=1, device_id=(inner_at(step), part), device_id_type=MESH
            )

    @pl.when(jnp.logical_not(outer))
    def _():
        pl.semaphore_wait(barrier, half - 1 + parts - 1)

    @pl.loop(0, inner)
    def _(step):
        pass_single(far_single(step))
        pass_single(near_single(step))

    @pl.when(jnp.logical_not(outer))
    def _():
        pl.semaphore_wait(ready, half)

    @pl.loop(0, doubles)
    def _(step):
        pass_double(double_at(step))

    def single_sent(step):
        matrix = far_single(step)
        dir_copy(matrix, 0, 0, single_owner(matrix), me).wait_send()

    @pl.when((me >= inner) & (me < groups - inner))
    def _():
        @pl.when(part == 0)
        def _():
            @pl.loop(0, inner)
            def _(step):
                single_sent(step)

            for peer in range(1, parts):
                pl.semaphore_signal(turn, inc=1, device_id=(me, peer), device_id_type=MESH)

        @pl.when(part > 0)
        def _():
            pl.semaphore_wait(turn, 1)

            @pl.loop(0, doubles)
            def _(step):
                send_double(double_at(step), 1 - upper)

    mom_copy = pltpu.make_async_copy(fresh, momentum_new, mom_sem)
    mom_copy.start()

    def result_copy(slot, group, matrix):
        return pltpu.make_async_remote_copy(
            src_ref=results.at[slot, group], dst_ref=update.at[matrix],
            send_sem=res_send.at[slot, group], recv_sem=res_recv.at[matrix],
            device_id=(group, part), device_id_type=MESH,
        )

    def own_copy(slot, matrix):
        return pltpu.make_async_copy(results.at[slot, me], update.at[matrix], own_sem.at[slot])

    def load_copy(slot, group, place):
        return pltpu.make_async_remote_copy(
            src_ref=load_tile.at[slot], dst_ref=loads.at[place],
            send_sem=load_send.at[slot, group], recv_sem=load_recv.at[place],
            device_id=(group, part), device_id_type=MESH,
        )

    def peer_copy(buffer, slot, peer, place, send, recv):
        return pltpu.make_async_remote_copy(
            src_ref=buffer.at[slot, place], dst_ref=buffer.at[slot, place],
            send_sem=send.at[slot, peer], recv_sem=recv.at[slot, place],
            device_id=(me, peer), device_id_type=MESH,
        )

    per_chunk = groups // chunks
    chunk_rows = KV_OUT // chunks

    @pl.loop(0, 2)
    def _(slot):
        matrix = jnp.where(slot == 0, me - inner, singles + my_double)
        active = ((slot == 0) & has_single) | ((slot == 1) & has_double)
        place = jnp.where(slot == 0, matrix, matrix + upper * doubles)
        served = jnp.where(slot == 0, groups, half)

        @pl.when(active)
        def _():
            blocks[slot, me] = dirs[matrix]
            row_ids = lax.broadcasted_iota(jnp.int32, (KV_OUT, KV_OUT), 0)
            col_ids = lax.broadcasted_iota(jnp.int32, (KV_OUT, KV_OUT), 1)

            @pl.loop(1, groups)
            def _(step):
                dir_copy(matrix, slot, 0, me, group_at(step)).wait_recv()

            whole = blocks[slot].reshape(KV_OUT, cols)
            partial_value = lax.dot_general(
                whole, whole, (((1,), (1,)), ((), ())), preferred_element_type=F32
            )
            grams[slot, part] = partial_value.astype(BF16)
            squares = jnp.sum(jnp.where(row_ids == col_ids, partial_value, 0.0))
            traces[slot, part] = jnp.full((8, 128), squares, F32)
            for step in range(1, parts):
                peer = lax.rem(part + step, parts)
                peer_copy(grams, slot, peer, part, gram_send, gram_recv).start()
                peer_copy(traces, slot, peer, part, trace_send, trace_recv).start()
            for step in range(1, parts):
                peer = lax.rem(part + step, parts)
                peer_copy(grams, slot, peer, peer, gram_send, gram_recv).wait_recv()
                peer_copy(traces, slot, peer, peer, trace_send, trace_recv).wait_recv()
            gram_sum = jnp.sum(grams[slot].astype(F32), axis=0)
            square_sum = jnp.sum(traces[slot], axis=0)[0:1, 0:1]
            scale = 1.0 / (jnp.sqrt(square_sum) + norm_eps)
            gram = (gram_sum * scale * scale).astype(BF16)
            gram_wide = gram.astype(F32)
            poly = coef_b * gram_wide + coef_c * mul(gram, gram)
            poly_first = poly.astype(BF16)
            mixed = mul(poly_first, gram)
            next_gram = (
                (coef_a * coef_a) * gram_wide
                + (2.0 * coef_a) * mixed
                + mul(mixed.astype(BF16), poly_first)
            ).astype(BF16)
            poly_second = (
                coef_b * next_gram.astype(F32) + coef_c * mul(next_gram, next_gram)
            )
            total = (
                coef_a * (poly_first.astype(F32) + poly_second)
                + mul(poly_second.astype(BF16), poly_first)
            )
            ident[...] = total.astype(BF16).reshape(ident.shape)
            out_scale = scale * math.sqrt(D)

            def chunk_at(step):
                forward = jnp.where(slot == 0, upper == 1, upper == 0)
                return jnp.where(forward, step, chunks - 1 - step)

            def send_chunk(first, start, stop):
                @pl.loop(start, stop)
                def _(member):
                    turned = jnp.where(first < half, per_chunk - member, member)
                    group = first + lax.rem(me + turned, per_chunk)
                    elsewhere(group, lambda: result_copy(slot, group, matrix).start())

                    @pl.when(group == me)
                    def _():
                        own_copy(slot, matrix).start()

            def chunk_body(step, square_total):
                first = chunk_at(step) * per_chunk
                mine = blocks[slot, pl.ds(first, per_chunk)].reshape(chunk_rows, cols)
                factor = ident[pl.ds(first, per_chunk)].reshape(chunk_rows, KV_OUT)
                values = (coef_a * coef_a) * mine.astype(F32) + mul(
                    factor, blocks[slot].reshape(KV_OUT, cols)
                )
                rounded = (out_scale * values).astype(BF16)
                results[slot, pl.ds(first, per_chunk)] = rounded.reshape(per_chunk, rows, cols)

                wide = rounded.astype(F32)
                squares = jnp.sum((wide * wide).reshape(chunk_rows // 8, 8, cols), axis=0)
                for lane in range(0, cols, 128):
                    square_total = square_total + squares[:, lane : lane + 128]

                @pl.when(step == last)
                def _():
                    load_tile[slot] = square_total
                    loads[place] = square_total

                    @pl.loop(1, groups)
                    def _(step):
                        load_copy(slot, group_at(step), place).start()

                    send_chunk(chunk_at(step - 1) * per_chunk, 0, per_chunk)

                send_chunk(first, 0, jnp.where(step == last - 1, 0, per_chunk))
                return square_total

            last = jnp.where(slot == 0, chunks, chunks // 2) - 1
            lax.fori_loop(0, last + 1, chunk_body, jnp.zeros((8, 128), F32))

    @pl.loop(0, singles)
    def _(matrix):
        elsewhere(single_owner(matrix), lambda: load_copy(0, me, matrix).wait_recv())

    @pl.loop(0, doubles)
    def _(index):
        for side in range(2):
            elsewhere(
                double_owner(index, side),
                lambda: load_copy(1, me, singles + index + side * doubles).wait_recv(),
            )

    owners_copy.wait()
    total_load = jnp.zeros((8, 128), F32)
    for matrix in range(mats):
        value = loads[matrix]
        if matrix >= singles:
            value = value + loads[matrix + doubles]
        total_load = total_load + jnp.where(owners[matrix] == me, 1.0, 0.0) * value
    halves[part] = jnp.full((8, 128), jnp.sum(total_load), F32)

    def half_copy(peer, place):
        return pltpu.make_async_remote_copy(
            src_ref=halves.at[place], dst_ref=halves.at[place],
            send_sem=half_send.at[peer], recv_sem=half_recv.at[place],
            device_id=(me, peer), device_id_type=MESH,
        )

    for step in range(1, parts):
        half_copy(lax.rem(part + step, parts), part).start()

    @pl.loop(0, 2)
    def _(slot):
        matrix = jnp.where(slot == 0, me - inner, singles + my_double)
        active = ((slot == 0) & has_single) | ((slot == 1) & has_double)
        place = jnp.where(slot == 0, matrix, matrix + upper * doubles)
        first = jnp.where(slot == 0, 0, upper * half)
        served = jnp.where(slot == 0, groups, half)

        @pl.when(active)
        def _():
            for step in range(1, parts):
                peer = lax.rem(part + step, parts)
                peer_copy(grams, slot, peer, part, gram_send, gram_recv).wait_send()
                peer_copy(traces, slot, peer, part, trace_send, trace_recv).wait_send()

            @pl.loop(0, served)
            def _(step):
                group = first + step
                elsewhere(group, lambda: result_copy(slot, group, matrix).wait_send())

            @pl.loop(1, groups)
            def _(step):
                load_copy(slot, group_at(step), place).wait_send()

            own_copy(slot, matrix).wait()

    @pl.loop(0, singles)
    def _(matrix):
        owner = single_owner(matrix)

        @pl.when(owner != me)
        def _():
            waited = ((me >= inner) & (me < groups - inner)) & (part == 0) & (lax.div(matrix, inner) != upper)
            waited = waited & (lax.rem(matrix - lax.rem(me, inner) + inner, inner) < inner)
            pl.when(jnp.logical_not(waited))(lambda: dir_copy(matrix, 0, 0, owner, me).wait_send())
            result_copy(0, me, matrix).wait_recv()

    @pl.loop(0, doubles)
    def _(index):
        matrix = singles + index
        for side in range(2):
            owner = double_owner(index, side)

            @pl.when(owner != me)
            def _():
                dir_copy(matrix, 1, side, owner, me).wait_send()

        elsewhere(
            double_owner(index, upper), lambda: result_copy(1, me, matrix).wait_recv()
        )

    for step in range(1, parts):
        peer = lax.rem(part + step, parts)
        half_copy(peer, part).wait_send()
        half_copy(peer, peer).wait_recv()
    owner_load[...] = jnp.sum(halves[...], axis=0) / (KV_OUT * D)
    mom_copy.wait()


def finish(
    update, momentum, load_block, norm_grads, norm_params, adam_m, adam_v,
    update_out, momentum_out, load_out, params_out, adam_m_out, adam_v_out,
    update_sem, momentum_sem,
):
    momentum_copy = pltpu.make_async_copy(momentum, momentum_out, momentum_sem)
    update_copy = pltpu.make_async_copy(update, update_out, update_sem)
    momentum_copy.start()
    update_copy.start()
    grad = norm_grads[...]
    adam_m_new = adam_first * adam_m[...] + (1.0 - adam_first) * grad
    adam_v_new = adam_second * adam_v[...] + (1.0 - adam_second) * grad * grad
    corrected = adam_m_new / first_fix / (jnp.sqrt(adam_v_new / second_fix) + adam_eps)
    params_out[...] = norm_params[...] - adam_rate * corrected
    adam_m_out[...] = adam_m_new
    adam_v_out[...] = adam_v_new
    load_out[0] = load_block[0, 0]
    momentum_copy.wait()
    update_copy.wait()


def on_device(groups, parts, grads, momentum, owners, norm_grads, norm_params, adam_m, adam_v):
    mats, rows, cols = grads.shape
    places = mats + (mats - groups // 2)
    dma = pltpu.SemaphoreType.DMA
    vmem = pl.BlockSpec(memory_space=pltpu.VMEM)
    hbm = pl.BlockSpec(memory_space=pl.ANY)
    update, momentum_new, load_block = pl.pallas_call(
        functools.partial(kernel, groups, parts, mats, 4),
        out_shape=(
            jax.ShapeDtypeStruct((mats, rows, cols), BF16),
            jax.ShapeDtypeStruct((mats, rows, cols), F32),
            jax.ShapeDtypeStruct((8, 128), F32),
        ),
        in_specs=[pl.BlockSpec(memory_space=pltpu.HBM)] * 3,
        out_specs=(hbm, hbm, vmem),
        scratch_shapes=[
            pltpu.VMEM((mats, rows, cols), BF16),
            pltpu.VMEM((2, groups, rows, cols), BF16),
            pltpu.VMEM((2, groups, rows, cols), BF16),
            pltpu.VMEM((2, parts, KV_OUT, KV_OUT), BF16),
            pltpu.VMEM((2, parts, 8, 128), F32),
            pltpu.VMEM((parts, 8, 128), F32),
            pltpu.VMEM((2, 8, 128), F32),
            pltpu.VMEM((places, 8, 128), F32),
            pltpu.VMEM((mats, rows, cols), F32),
            pltpu.VMEM((groups, rows, KV_OUT), BF16),
            dma((mats, 2)), dma((2, groups)), dma((2, groups)), dma((mats,)),
            dma((2, parts)), dma((2, parts)), dma((2, parts)), dma((2, parts)),
            dma((parts,)), dma((parts,)), dma((2, groups)), dma((places,)),
            dma((2,)), dma, pltpu.SemaphoreType.REGULAR, pltpu.SemaphoreType.REGULAR,
            pltpu.SMEM((mats,), jnp.int32),
            pltpu.VMEM((mats, rows, cols), BF16),
            pltpu.VMEM((mats, rows, cols), F32),
            dma, dma((mats,)), dma((mats,)),
        ],
        compiler_params=pltpu.CompilerParams(
            collective_id=0, has_side_effects=True, vmem_limit_bytes=28 * 1024 * 1024
        ),
    )(*(pltpu.with_memory_space_constraint(array, pltpu.HBM) for array in (owners, grads, momentum)))
    norm_shape = jax.ShapeDtypeStruct(norm_grads.shape, F32)
    update, momentum_new, owner_load, norm_params_new, adam_m_new, adam_v_new = pl.pallas_call(
        finish,
        out_shape=(
            jax.ShapeDtypeStruct(update.shape, BF16),
            jax.ShapeDtypeStruct(momentum_new.shape, F32),
            jax.ShapeDtypeStruct((1,), F32),
            norm_shape, norm_shape, norm_shape,
        ),
        in_specs=[hbm, hbm] + [vmem] * 5,
        out_specs=(
            pl.BlockSpec(memory_space=pltpu.HBM), pl.BlockSpec(memory_space=pltpu.HBM),
            pl.BlockSpec(memory_space=pltpu.SMEM), vmem, vmem, vmem,
        ),
        scratch_shapes=[dma, dma],
        compiler_params=pltpu.CompilerParams(vmem_limit_bytes=8 * 1024 * 1024),
    )(update, momentum_new, load_block, norm_grads, norm_params, adam_m, adam_v)
    return (update, momentum_new, owner_load, norm_params_new, adam_m_new, adam_v_new)


def solution(mesh):
    return jax.shard_map(
        functools.partial(on_device, mesh.shape["wide"], mesh.shape["narrow"]),
        mesh=mesh,
        in_specs=(
            P(None, "wide", "narrow"),
            P(None, "wide", "narrow"),
            P(),
            P("narrow", "wide"),
            P("narrow", "wide"),
            P("narrow", "wide"),
            P("narrow", "wide"),
        ),
        out_specs=(
            P(None, "wide", "narrow"),
            P(None, "wide", "narrow"),
            P("wide"),
            P("narrow", "wide"),
            P("narrow", "wide"),
            P("narrow", "wide"),
        ),
        check_vma=False,
    )
```

```python
import functools
import math

import jax
import jax.numpy as jnp
from jax import lax
from jax.experimental import pallas as pl
from jax.experimental.pallas import tpu as pltpu
from jax.sharding import PartitionSpec as P

D = 2048
KV_OUT = 512

coef_a = 3.4445
coef_b = -4.775
coef_c = 2.0315
muon_beta = 0.95
norm_eps = 1e-07
adam_first = 0.9
adam_second = 0.95
adam_rate = 0.02
adam_eps = 1e-08
first_fix = 1.0 - 0.9**10
second_fix = 1.0 - 0.95**10

MESH = pl.DeviceIdType.MESH
BF16 = jnp.bfloat16
F32 = jnp.float32


def mul(left, right):
    return jnp.dot(left, right, preferred_element_type=F32)


def kernel(
    groups, parts, mats, chunks,
    owners_hbm, grads_hbm, momentum_hbm,
    update, momentum_new, owner_load,
    dirs, blocks, results, grams, traces, halves, load_tile, loads, fresh, ident,
    dir_send, dir_recv, res_send, res_recv, gram_send, gram_recv,
    trace_send, trace_recv, half_send, half_recv, load_send, load_recv, own_sem, mom_sem, turn, ready,
    owners, grads, momentum, owners_sem, grads_sem, momentum_sem,
):
    me = lax.axis_index("wide")
    part = lax.axis_index("narrow")
    rows, cols = dirs.shape[1], dirs.shape[2]
    half = groups // 2
    inner = half // 2
    singles = half
    doubles = mats - singles
    upper = lax.div(me, half)

    def single_owner(matrix):
        return inner + matrix

    def double_owner(index, side):
        return jnp.where(side == 0, index, groups - 1 - index)

    my_double = jnp.where(upper == 0, me, groups - 1 - me)
    has_single = (me >= inner) & (me < inner + singles)
    has_double = my_double < doubles

    def group_at(step):
        return lax.rem(me + step, groups)

    def elsewhere(group, body):
        pl.when(group != me)(body)

    def loads_of(matrix):
        return (
            pltpu.make_async_copy(grads_hbm.at[matrix], grads.at[matrix], grads_sem.at[matrix]),
            pltpu.make_async_copy(
                momentum_hbm.at[matrix], momentum.at[matrix], momentum_sem.at[matrix]
            ),
        )

    def far_single(step):
        return (1 - upper) * inner + lax.rem(me + step, inner)

    def near_single(step):
        return upper * inner + lax.rem(me + step, inner)

    extra = doubles - inner

    def double_at(step):
        return jnp.where(
            step < inner, lax.rem(me + step, inner), inner + lax.rem(step + me, extra)
        )

    def fetch(matrix):
        for copy in loads_of(matrix):
            copy.start()

    owners_copy = pltpu.make_async_copy(owners_hbm, owners, owners_sem)
    barrier = pltpu.get_barrier_semaphore()
    outer = (me < inner) | (me >= groups - inner)

    def inner_at(step):
        return inner + lax.rem(lax.rem(me + inner, half) + step, half)

    @pl.loop(1, groups)
    def _(step):
        group = group_at(step)
        group_outer = (group < inner) | (group >= groups - inner)

        @pl.when(group_outer | jnp.logical_not(outer))
        def _():
            pl.semaphore_signal(barrier, inc=1, device_id=(group, part), device_id_type=MESH)

    for step in range(1, parts):
        peer = lax.rem(part + step, parts)
        pl.semaphore_signal(barrier, inc=1, device_id=(me, peer), device_id_type=MESH)

    @pl.loop(0, inner)
    def _(step):
        fetch(far_single(step))
        fetch(near_single(step))

    @pl.loop(0, doubles)
    def _(step):
        fetch(singles + double_at(step))


    owners_copy.start()

    def dir_copy(matrix, slot, which, group, source):
        return pltpu.make_async_remote_copy(
            src_ref=dirs.at[matrix], dst_ref=blocks.at[slot, source],
            send_sem=dir_send.at[matrix, which], recv_sem=dir_recv.at[slot, source],
            device_id=(group, part), device_id_type=MESH,
        )

    def direct(matrix):
        for copy in loads_of(matrix):
            copy.wait()
        grad_values = grads[matrix].astype(F32)
        new = muon_beta * momentum[matrix] + grad_values
        fresh[matrix] = new
        dirs[matrix] = (grad_values + muon_beta * new).astype(BF16)

    def send_single(matrix):
        owner = single_owner(matrix)
        elsewhere(owner, lambda: dir_copy(matrix, 0, 0, owner, me).start())

    def send_double(index, side):
        owner = double_owner(index, side)
        elsewhere(owner, lambda: dir_copy(singles + index, 1, side, owner, me).start())

    def pass_single(matrix):
        direct(matrix)
        send_single(matrix)

    def pass_double(index):
        direct(singles + index)
        pl.when(jnp.logical_not(((me >= inner) & (me < groups - inner)) & (part > 0)))(lambda: send_double(index, 1 - upper))
        send_double(index, upper)

    @pl.when(outer)
    def _():
        pl.semaphore_wait(barrier, groups - 1 + parts - 1)

        @pl.loop(0, half)
        def _(step):
            pl.semaphore_signal(
                ready, inc=1, device_id=(inner_at(step), part), device_id_type=MESH
            )

    @pl.when(jnp.logical_not(outer))
    def _():
        pl.semaphore_wait(barrier, half - 1 + parts - 1)

    @pl.loop(0, inner)
    def _(step):
        pass_single(far_single(step))

    @pl.loop(0, inner)
    def _(step):
        pass_single(near_single(step))

    @pl.when(jnp.logical_not(outer))
    def _():
        pl.semaphore_wait(ready, half)

    @pl.loop(0, doubles)
    def _(step):
        pass_double(double_at(step))

    def single_sent(step):
        matrix = far_single(step)
        dir_copy(matrix, 0, 0, single_owner(matrix), me).wait_send()

    @pl.when((me >= inner) & (me < groups - inner))
    def _():
        @pl.when(part == 0)
        def _():
            @pl.loop(0, inner)
            def _(step):
                single_sent(step)

            for peer in range(1, parts):
                pl.semaphore_signal(turn, inc=1, device_id=(me, peer), device_id_type=MESH)

        @pl.when(part > 0)
        def _():
            pl.semaphore_wait(turn, 1)

            @pl.loop(0, doubles)
            def _(step):
                send_double(double_at(step), 1 - upper)

    mom_copy = pltpu.make_async_copy(fresh, momentum_new, mom_sem)
    mom_copy.start()

    def result_copy(slot, group, matrix):
        return pltpu.make_async_remote_copy(
            src_ref=results.at[slot, group], dst_ref=update.at[matrix],
            send_sem=res_send.at[slot, group], recv_sem=res_recv.at[matrix],
            device_id=(group, part), device_id_type=MESH,
        )

    def own_copy(slot, matrix):
        return pltpu.make_async_copy(results.at[slot, me], update.at[matrix], own_sem.at[slot])

    def load_copy(slot, group, place):
        return pltpu.make_async_remote_copy(
            src_ref=load_tile.at[slot], dst_ref=loads.at[place],
            send_sem=load_send.at[slot, group], recv_sem=load_recv.at[place],
            device_id=(group, part), device_id_type=MESH,
        )

    def peer_copy(buffer, slot, peer, place, send, recv):
        return pltpu.make_async_remote_copy(
            src_ref=buffer.at[slot, place], dst_ref=buffer.at[slot, place],
            send_sem=send.at[slot, peer], recv_sem=recv.at[slot, place],
            device_id=(me, peer), device_id_type=MESH,
        )

    per_chunk = groups // chunks
    chunk_rows = KV_OUT // chunks

    @pl.loop(0, 2)
    def _(slot):
        matrix = jnp.where(slot == 0, me - inner, singles + my_double)
        active = ((slot == 0) & has_single) | ((slot == 1) & has_double)
        place = jnp.where(slot == 0, matrix, matrix + upper * doubles)
        served = jnp.where(slot == 0, groups, half)

        @pl.when(active)
        def _():
            blocks[slot, me] = dirs[matrix]
            row_ids = lax.broadcasted_iota(jnp.int32, (KV_OUT, KV_OUT), 0)
            col_ids = lax.broadcasted_iota(jnp.int32, (KV_OUT, KV_OUT), 1)

            @pl.loop(1, groups)
            def _(step):
                dir_copy(matrix, slot, 0, me, group_at(step)).wait_recv()

            whole = blocks[slot].reshape(KV_OUT, cols)
            partial_value = lax.dot_general(
                whole, whole, (((1,), (1,)), ((), ())), preferred_element_type=F32
            )
            grams[slot, part] = partial_value.astype(BF16)
            squares = jnp.sum(jnp.where(row_ids == col_ids, partial_value, 0.0))
            traces[slot, part] = jnp.full((8, 128), squares, F32)
            for step in range(1, parts):
                peer = lax.rem(part + step, parts)
                peer_copy(grams, slot, peer, part, gram_send, gram_recv).start()
                peer_copy(traces, slot, peer, part, trace_send, trace_recv).start()
            for step in range(1, parts):
                peer = lax.rem(part + step, parts)
                peer_copy(grams, slot, peer, peer, gram_send, gram_recv).wait_recv()
                peer_copy(traces, slot, peer, peer, trace_send, trace_recv).wait_recv()
            gram_sum = jnp.sum(grams[slot].astype(F32), axis=0)
            square_sum = jnp.sum(traces[slot], axis=0)[0:1, 0:1]
            scale = 1.0 / (jnp.sqrt(square_sum) + norm_eps)
            gram = (gram_sum * scale * scale).astype(BF16)
            gram_wide = gram.astype(F32)
            poly = coef_b * gram_wide + coef_c * mul(gram, gram)
            poly_first = poly.astype(BF16)
            mixed = mul(poly_first, gram)
            next_gram = (
                (coef_a * coef_a) * gram_wide
                + (2.0 * coef_a) * mixed
                + mul(mixed.astype(BF16), poly_first)
            ).astype(BF16)
            poly_second = (
                coef_b * next_gram.astype(F32) + coef_c * mul(next_gram, next_gram)
            )
            total = (
                coef_a * (poly_first.astype(F32) + poly_second)
                + mul(poly_second.astype(BF16), poly_first)
            )
            ident[...] = total.astype(BF16).reshape(ident.shape)
            out_scale = scale * math.sqrt(D)

            def chunk_at(step):
                forward = jnp.where(slot == 0, upper == 1, upper == 0)
                return jnp.where(forward, step, chunks - 1 - step)

            def send_chunk(first, start, stop):
                @pl.loop(start, stop)
                def _(member):
                    turned = jnp.where(first < half, per_chunk - member, member)
                    group = first + lax.rem(me + turned, per_chunk)
                    elsewhere(group, lambda: result_copy(slot, group, matrix).start())

                    @pl.when(group == me)
                    def _():
                        own_copy(slot, matrix).start()

            def chunk_body(step, square_total):
                first = chunk_at(step) * per_chunk
                mine = blocks[slot, pl.ds(first, per_chunk)].reshape(chunk_rows, cols)
                factor = ident[pl.ds(first, per_chunk)].reshape(chunk_rows, KV_OUT)
                values = (coef_a * coef_a) * mine.astype(F32) + mul(
                    factor, blocks[slot].reshape(KV_OUT, cols)
                )
                rounded = (out_scale * values).astype(BF16)
                results[slot, pl.ds(first, per_chunk)] = rounded.reshape(per_chunk, rows, cols)

                wide = rounded.astype(F32)
                squares = jnp.sum((wide * wide).reshape(chunk_rows // 8, 8, cols), axis=0)
                for lane in range(0, cols, 128):
                    square_total = square_total + squares[:, lane : lane + 128]

                @pl.when(step == last)
                def _():
                    load_tile[slot] = square_total
                    loads[place] = square_total

                    @pl.loop(1, groups)
                    def _(step):
                        load_copy(slot, group_at(step), place).start()

                    send_chunk(chunk_at(step - 1) * per_chunk, 0, per_chunk)

                send_chunk(first, 0, jnp.where(step == last - 1, 0, per_chunk))
                return square_total

            last = jnp.where(slot == 0, chunks, chunks // 2) - 1
            lax.fori_loop(0, last + 1, chunk_body, jnp.zeros((8, 128), F32))

    @pl.loop(0, singles)
    def _(matrix):
        elsewhere(single_owner(matrix), lambda: load_copy(0, me, matrix).wait_recv())

    @pl.loop(0, doubles)
    def _(index):
        for side in range(2):
            elsewhere(
                double_owner(index, side),
                lambda: load_copy(1, me, singles + index + side * doubles).wait_recv(),
            )

    owners_copy.wait()
    total_load = jnp.zeros((8, 128), F32)
    for matrix in range(mats):
        value = loads[matrix]
        if matrix >= singles:
            value = value + loads[matrix + doubles]
        total_load = total_load + jnp.where(owners[matrix] == me, 1.0, 0.0) * value
    halves[part] = jnp.full((8, 128), jnp.sum(total_load), F32)

    def half_copy(peer, place):
        return pltpu.make_async_remote_copy(
            src_ref=halves.at[place], dst_ref=halves.at[place],
            send_sem=half_send.at[peer], recv_sem=half_recv.at[place],
            device_id=(me, peer), device_id_type=MESH,
        )

    for step in range(1, parts):
        half_copy(lax.rem(part + step, parts), part).start()

    @pl.loop(0, 2)
    def _(slot):
        matrix = jnp.where(slot == 0, me - inner, singles + my_double)
        active = ((slot == 0) & has_single) | ((slot == 1) & has_double)
        place = jnp.where(slot == 0, matrix, matrix + upper * doubles)
        first = jnp.where(slot == 0, 0, upper * half)
        served = jnp.where(slot == 0, groups, half)

        @pl.when(active)
        def _():
            for step in range(1, parts):
                peer = lax.rem(part + step, parts)
                peer_copy(grams, slot, peer, part, gram_send, gram_recv).wait_send()
                peer_copy(traces, slot, peer, part, trace_send, trace_recv).wait_send()

            @pl.loop(0, served)
            def _(step):
                group = first + step
                elsewhere(group, lambda: result_copy(slot, group, matrix).wait_send())

            @pl.loop(1, groups)
            def _(step):
                load_copy(slot, group_at(step), place).wait_send()

            own_copy(slot, matrix).wait()

    @pl.loop(0, singles)
    def _(matrix):
        owner = single_owner(matrix)

        @pl.when(owner != me)
        def _():
            waited = ((me >= inner) & (me < groups - inner)) & (part == 0) & (lax.div(matrix, inner) != upper)
            waited = waited & (lax.rem(matrix - lax.rem(me, inner) + inner, inner) < inner)
            pl.when(jnp.logical_not(waited))(lambda: dir_copy(matrix, 0, 0, owner, me).wait_send())
            result_copy(0, me, matrix).wait_recv()

    @pl.loop(0, doubles)
    def _(index):
        matrix = singles + index
        for side in range(2):
            owner = double_owner(index, side)

            @pl.when(owner != me)
            def _():
                dir_copy(matrix, 1, side, owner, me).wait_send()

        elsewhere(
            double_owner(index, upper), lambda: result_copy(1, me, matrix).wait_recv()
        )

    for step in range(1, parts):
        peer = lax.rem(part + step, parts)
        half_copy(peer, part).wait_send()
        half_copy(peer, peer).wait_recv()
    owner_load[...] = jnp.sum(halves[...], axis=0) / (KV_OUT * D)
    mom_copy.wait()


def finish(
    update, momentum, load_block, norm_grads, norm_params, adam_m, adam_v,
    update_out, momentum_out, load_out, params_out, adam_m_out, adam_v_out,
    update_sem, momentum_sem,
):
    mats = momentum.shape[0]
    cuts = [mats * piece // 2 for piece in range(2 + 1)]
    copies = [
        pltpu.make_async_copy(
            source.at[pl.ds(start, stop - start)], target.at[pl.ds(start, stop - start)],
            sem.at[piece],
        )
        for source, target, sem in (
            (momentum, momentum_out, momentum_sem), (update, update_out, update_sem)
        )
        for piece, (start, stop) in enumerate(zip(cuts, cuts[1:]))
    ]
    for copy in copies:
        copy.start()
    grad = norm_grads[...]
    adam_m_new = adam_first * adam_m[...] + (1.0 - adam_first) * grad
    adam_v_new = adam_second * adam_v[...] + (1.0 - adam_second) * grad * grad
    corrected = adam_m_new / first_fix / (jnp.sqrt(adam_v_new / second_fix) + adam_eps)
    params_out[...] = norm_params[...] - adam_rate * corrected
    adam_m_out[...] = adam_m_new
    adam_v_out[...] = adam_v_new
    load_out[0] = load_block[0, 0]
    for copy in copies:
        copy.wait()


def on_device(groups, parts, grads, momentum, owners, norm_grads, norm_params, adam_m, adam_v):
    mats, rows, cols = grads.shape
    places = mats + (mats - groups // 2)
    dma = pltpu.SemaphoreType.DMA
    vmem = pl.BlockSpec(memory_space=pltpu.VMEM)
    hbm = pl.BlockSpec(memory_space=pl.ANY)
    update, momentum_new, load_block = pl.pallas_call(
        functools.partial(kernel, groups, parts, mats, 4),
        out_shape=(
            jax.ShapeDtypeStruct((mats, rows, cols), BF16),
            jax.ShapeDtypeStruct((mats, rows, cols), F32),
            jax.ShapeDtypeStruct((8, 128), F32),
        ),
        in_specs=[pl.BlockSpec(memory_space=pltpu.HBM)] * 3,
        out_specs=(hbm, hbm, vmem),
        scratch_shapes=[
            pltpu.VMEM((mats, rows, cols), BF16),
            pltpu.VMEM((2, groups, rows, cols), BF16),
            pltpu.VMEM((2, groups, rows, cols), BF16),
            pltpu.VMEM((2, parts, KV_OUT, KV_OUT), BF16),
            pltpu.VMEM((2, parts, 8, 128), F32),
            pltpu.VMEM((parts, 8, 128), F32),
            pltpu.VMEM((2, 8, 128), F32),
            pltpu.VMEM((places, 8, 128), F32),
            pltpu.VMEM((mats, rows, cols), F32),
            pltpu.VMEM((groups, rows, KV_OUT), BF16),
            dma((mats, 2)), dma((2, groups)), dma((2, groups)), dma((mats,)),
            dma((2, parts)), dma((2, parts)), dma((2, parts)), dma((2, parts)),
            dma((parts,)), dma((parts,)), dma((2, groups)), dma((places,)),
            dma((2,)), dma, pltpu.SemaphoreType.REGULAR, pltpu.SemaphoreType.REGULAR,
            pltpu.SMEM((mats,), jnp.int32),
            pltpu.VMEM((mats, rows, cols), BF16),
            pltpu.VMEM((mats, rows, cols), F32),
            dma, dma((mats,)), dma((mats,)),
        ],
        compiler_params=pltpu.CompilerParams(
            collective_id=0, has_side_effects=True, vmem_limit_bytes=28 * 1024 * 1024
        ),
    )(*(pltpu.with_memory_space_constraint(array, pltpu.HBM) for array in (owners, grads, momentum)))
    norm_shape = jax.ShapeDtypeStruct(norm_grads.shape, F32)
    update, momentum_new, owner_load, norm_params_new, adam_m_new, adam_v_new = pl.pallas_call(
        finish,
        out_shape=(
            jax.ShapeDtypeStruct(update.shape, BF16),
            jax.ShapeDtypeStruct(momentum_new.shape, F32),
            jax.ShapeDtypeStruct((1,), F32),
            norm_shape, norm_shape, norm_shape,
        ),
        in_specs=[hbm, hbm] + [vmem] * 5,
        out_specs=(
            pl.BlockSpec(memory_space=pltpu.HBM), pl.BlockSpec(memory_space=pltpu.HBM),
            pl.BlockSpec(memory_space=pltpu.SMEM), vmem, vmem, vmem,
        ),
        scratch_shapes=[dma((2,)), dma((2,))],
        compiler_params=pltpu.CompilerParams(vmem_limit_bytes=8 * 1024 * 1024),
    )(update, momentum_new, load_block, norm_grads, norm_params, adam_m, adam_v)
    return (update, momentum_new, owner_load, norm_params_new, adam_m_new, adam_v_new)


def solution(mesh):
    return jax.shard_map(
        functools.partial(on_device, mesh.shape["wide"], mesh.shape["narrow"]),
        mesh=mesh,
        in_specs=(
            P(None, "wide", "narrow"),
            P(None, "wide", "narrow"),
            P(),
            P("narrow", "wide"),
            P("narrow", "wide"),
            P("narrow", "wide"),
            P("narrow", "wide"),
        ),
        out_specs=(
            P(None, "wide", "narrow"),
            P(None, "wide", "narrow"),
            P("wide"),
            P("narrow", "wide"),
            P("narrow", "wide"),
            P("narrow", "wide"),
        ),
        check_vma=False,
    )
```

```python
import functools
import math

import jax
import jax.numpy as jnp
from jax import lax
from jax.experimental import pallas as pl
from jax.experimental.pallas import tpu as pltpu
from jax.sharding import PartitionSpec as P

D = 2048
KV_OUT = 512

coef_a = 3.4445
coef_b = -4.775
coef_c = 2.0315
muon_beta = 0.95
norm_eps = 1e-07
adam_first = 0.9
adam_second = 0.95
adam_rate = 0.02
adam_eps = 1e-08
first_fix = 1.0 - 0.9**10
second_fix = 1.0 - 0.95**10

MESH = pl.DeviceIdType.MESH
BF16 = jnp.bfloat16
F32 = jnp.float32


def mul(left, right):
    return jnp.dot(left, right, preferred_element_type=F32)


def kernel(
    groups, parts, mats, chunks,
    owners_hbm, grads_hbm, momentum_hbm,
    update, momentum_new, owner_load,
    dirs, blocks, results, grams, traces, halves, load_tile, loads, fresh, ident,
    dir_send, dir_recv, res_send, res_recv, gram_send, gram_recv,
    trace_send, trace_recv, half_send, half_recv, load_send, load_recv, own_sem, mom_sem, turn, ready,
    owners, grads, momentum, owners_sem, grads_sem, momentum_sem,
):
    me = lax.axis_index("wide")
    part = lax.axis_index("narrow")
    rows, cols = dirs.shape[1], dirs.shape[2]
    half = groups // 2
    inner = half // 2
    singles = half
    doubles = mats - singles
    upper = lax.div(me, half)

    def single_owner(matrix):
        return inner + matrix

    def double_owner(index, side):
        return jnp.where(side == 0, index, groups - 1 - index)

    my_double = jnp.where(upper == 0, me, groups - 1 - me)
    has_single = (me >= inner) & (me < inner + singles)
    has_double = my_double < doubles

    def group_at(step):
        return lax.rem(me + step, groups)

    def elsewhere(group, body):
        pl.when(group != me)(body)

    def loads_of(matrix):
        return (
            pltpu.make_async_copy(grads_hbm.at[matrix], grads.at[matrix], grads_sem.at[matrix]),
            pltpu.make_async_copy(
                momentum_hbm.at[matrix], momentum.at[matrix], momentum_sem.at[matrix]
            ),
        )

    def far_single(step):
        return (1 - upper) * inner + lax.rem(me + step, inner)

    def near_single(step):
        return upper * inner + lax.rem(me + step, inner)

    extra = doubles - inner

    def double_at(step):
        return jnp.where(
            step < inner, lax.rem(me + step, inner), inner + lax.rem(step + me, extra)
        )

    def fetch(matrix):
        for copy in loads_of(matrix):
            copy.start()

    owners_copy = pltpu.make_async_copy(owners_hbm, owners, owners_sem)
    barrier = pltpu.get_barrier_semaphore()
    outer = (me < inner) | (me >= groups - inner)

    def inner_at(step):
        return inner + lax.rem(lax.rem(me + inner, half) + step, half)

    @pl.loop(1, groups)
    def _(step):
        group = group_at(step)
        group_outer = (group < inner) | (group >= groups - inner)

        @pl.when(group_outer | jnp.logical_not(outer))
        def _():
            pl.semaphore_signal(barrier, inc=1, device_id=(group, part), device_id_type=MESH)

    for step in range(1, parts):
        peer = lax.rem(part + step, parts)
        pl.semaphore_signal(barrier, inc=1, device_id=(me, peer), device_id_type=MESH)

    @pl.loop(0, inner)
    def _(step):
        fetch(far_single(step))

    @pl.loop(0, inner)
    def _(step):
        fetch(near_single(step))

    @pl.loop(0, doubles)
    def _(step):
        fetch(singles + double_at(step))


    owners_copy.start()

    def dir_copy(matrix, slot, which, group, source):
        return pltpu.make_async_remote_copy(
            src_ref=dirs.at[matrix], dst_ref=blocks.at[slot, source],
            send_sem=dir_send.at[matrix, which], recv_sem=dir_recv.at[slot, source],
            device_id=(group, part), device_id_type=MESH,
        )

    def direct(matrix):
        for copy in loads_of(matrix):
            copy.wait()
        grad_values = grads[matrix].astype(F32)
        new = muon_beta * momentum[matrix] + grad_values
        fresh[matrix] = new
        dirs[matrix] = (grad_values + muon_beta * new).astype(BF16)

    def send_single(matrix):
        owner = single_owner(matrix)
        elsewhere(owner, lambda: dir_copy(matrix, 0, 0, owner, me).start())

    def send_double(index, side):
        owner = double_owner(index, side)
        elsewhere(owner, lambda: dir_copy(singles + index, 1, side, owner, me).start())

    def pass_single(matrix):
        direct(matrix)
        send_single(matrix)

    def pass_double(index):
        direct(singles + index)
        pl.when(jnp.logical_not(((me >= inner) & (me < groups - inner)) & (part > 0)))(lambda: send_double(index, 1 - upper))
        send_double(index, upper)

    ahead = 2

    @pl.loop(0, ahead)
    def _(step):
        direct(far_single(step))

    @pl.when(outer)
    def _():
        pl.semaphore_wait(barrier, groups - 1 + parts - 1)

        @pl.loop(0, half)
        def _(step):
            pl.semaphore_signal(
                ready, inc=1, device_id=(inner_at(step), part), device_id_type=MESH
            )

    @pl.when(jnp.logical_not(outer))
    def _():
        pl.semaphore_wait(barrier, half - 1 + parts - 1)

    @pl.loop(0, ahead)
    def _(step):
        send_single(far_single(step))

    @pl.loop(ahead, inner)
    def _(step):
        pass_single(far_single(step))

    @pl.loop(0, inner)
    def _(step):
        pass_single(near_single(step))

    @pl.when(jnp.logical_not(outer))
    def _():
        pl.semaphore_wait(ready, half)

    @pl.loop(0, doubles)
    def _(step):
        pass_double(double_at(step))

    def single_sent(step):
        matrix = far_single(step)
        dir_copy(matrix, 0, 0, single_owner(matrix), me).wait_send()

    @pl.when((me >= inner) & (me < groups - inner))
    def _():
        @pl.when(part == 0)
        def _():
            @pl.loop(0, inner)
            def _(step):
                single_sent(step)

            for peer in range(1, parts):
                pl.semaphore_signal(turn, inc=1, device_id=(me, peer), device_id_type=MESH)

        @pl.when(part > 0)
        def _():
            pl.semaphore_wait(turn, 1)

            @pl.loop(0, doubles)
            def _(step):
                send_double(double_at(step), 1 - upper)

    mom_copy = pltpu.make_async_copy(fresh, momentum_new, mom_sem)
    mom_copy.start()

    def result_copy(slot, group, matrix):
        return pltpu.make_async_remote_copy(
            src_ref=results.at[slot, group], dst_ref=update.at[matrix],
            send_sem=res_send.at[slot, group], recv_sem=res_recv.at[matrix],
            device_id=(group, part), device_id_type=MESH,
        )

    def own_copy(slot, matrix):
        return pltpu.make_async_copy(results.at[slot, me], update.at[matrix], own_sem.at[slot])

    def load_copy(slot, group, place):
        return pltpu.make_async_remote_copy(
            src_ref=load_tile.at[slot], dst_ref=loads.at[place],
            send_sem=load_send.at[slot, group], recv_sem=load_recv.at[place],
            device_id=(group, part), device_id_type=MESH,
        )

    def peer_copy(buffer, slot, peer, place, send, recv):
        return pltpu.make_async_remote_copy(
            src_ref=buffer.at[slot, place], dst_ref=buffer.at[slot, place],
            send_sem=send.at[slot, peer], recv_sem=recv.at[slot, place],
            device_id=(me, peer), device_id_type=MESH,
        )

    per_chunk = groups // chunks
    chunk_rows = KV_OUT // chunks

    @pl.loop(0, 2)
    def _(slot):
        matrix = jnp.where(slot == 0, me - inner, singles + my_double)
        active = ((slot == 0) & has_single) | ((slot == 1) & has_double)
        place = jnp.where(slot == 0, matrix, matrix + upper * doubles)
        served = jnp.where(slot == 0, groups, half)

        @pl.when(active)
        def _():
            blocks[slot, me] = dirs[matrix]
            row_ids = lax.broadcasted_iota(jnp.int32, (KV_OUT, KV_OUT), 0)
            col_ids = lax.broadcasted_iota(jnp.int32, (KV_OUT, KV_OUT), 1)

            @pl.loop(1, groups)
            def _(step):
                dir_copy(matrix, slot, 0, me, group_at(step)).wait_recv()

            whole = blocks[slot].reshape(KV_OUT, cols)
            partial_value = lax.dot_general(
                whole, whole, (((1,), (1,)), ((), ())), preferred_element_type=F32
            )
            grams[slot, part] = partial_value.astype(BF16)
            squares = jnp.sum(jnp.where(row_ids == col_ids, partial_value, 0.0))
            traces[slot, part] = jnp.full((8, 128), squares, F32)
            for step in range(1, parts):
                peer = lax.rem(part + step, parts)
                peer_copy(grams, slot, peer, part, gram_send, gram_recv).start()
                peer_copy(traces, slot, peer, part, trace_send, trace_recv).start()
            for step in range(1, parts):
                peer = lax.rem(part + step, parts)
                peer_copy(grams, slot, peer, peer, gram_send, gram_recv).wait_recv()
                peer_copy(traces, slot, peer, peer, trace_send, trace_recv).wait_recv()
            gram_sum = jnp.sum(grams[slot].astype(F32), axis=0)
            square_sum = jnp.sum(traces[slot], axis=0)[0:1, 0:1]
            scale = 1.0 / (jnp.sqrt(square_sum) + norm_eps)
            gram = (gram_sum * scale * scale).astype(BF16)
            gram_wide = gram.astype(F32)
            poly = coef_b * gram_wide + coef_c * mul(gram, gram)
            poly_first = poly.astype(BF16)
            mixed = mul(poly_first, gram)
            next_gram = (
                (coef_a * coef_a) * gram_wide
                + (2.0 * coef_a) * mixed
                + mul(mixed.astype(BF16), poly_first)
            ).astype(BF16)
            poly_second = (
                coef_b * next_gram.astype(F32) + coef_c * mul(next_gram, next_gram)
            )
            total = (
                coef_a * (poly_first.astype(F32) + poly_second)
                + mul(poly_second.astype(BF16), poly_first)
            )
            ident[...] = total.astype(BF16).reshape(ident.shape)
            out_scale = scale * math.sqrt(D)

            def chunk_at(step):
                forward = jnp.where(slot == 0, upper == 1, upper == 0)
                return jnp.where(forward, step, chunks - 1 - step)

            def send_chunk(first, start, stop):
                @pl.loop(start, stop)
                def _(member):
                    turned = jnp.where(first < half, per_chunk - member, member)
                    group = first + lax.rem(me + turned, per_chunk)
                    elsewhere(group, lambda: result_copy(slot, group, matrix).start())

                    @pl.when(group == me)
                    def _():
                        own_copy(slot, matrix).start()

            def chunk_body(step, square_total):
                first = chunk_at(step) * per_chunk
                mine = blocks[slot, pl.ds(first, per_chunk)].reshape(chunk_rows, cols)
                factor = ident[pl.ds(first, per_chunk)].reshape(chunk_rows, KV_OUT)
                values = (coef_a * coef_a) * mine.astype(F32) + mul(
                    factor, blocks[slot].reshape(KV_OUT, cols)
                )
                rounded = (out_scale * values).astype(BF16)
                results[slot, pl.ds(first, per_chunk)] = rounded.reshape(per_chunk, rows, cols)

                wide = rounded.astype(F32)
                squares = jnp.sum((wide * wide).reshape(chunk_rows // 8, 8, cols), axis=0)
                for lane in range(0, cols, 128):
                    square_total = square_total + squares[:, lane : lane + 128]

                @pl.when(step == last)
                def _():
                    load_tile[slot] = square_total
                    loads[place] = square_total

                    @pl.loop(1, groups)
                    def _(step):
                        load_copy(slot, group_at(step), place).start()

                    send_chunk(chunk_at(step - 1) * per_chunk, 0, per_chunk)

                send_chunk(first, 0, jnp.where(step == last - 1, 0, per_chunk))
                return square_total

            last = jnp.where(slot == 0, chunks, chunks // 2) - 1
            lax.fori_loop(0, last + 1, chunk_body, jnp.zeros((8, 128), F32))

    @pl.loop(0, singles)
    def _(matrix):
        elsewhere(single_owner(matrix), lambda: load_copy(0, me, matrix).wait_recv())

    @pl.loop(0, doubles)
    def _(index):
        for side in range(2):
            elsewhere(
                double_owner(index, side),
                lambda: load_copy(1, me, singles + index + side * doubles).wait_recv(),
            )

    owners_copy.wait()
    total_load = jnp.zeros((8, 128), F32)
    for matrix in range(mats):
        value = loads[matrix]
        if matrix >= singles:
            value = value + loads[matrix + doubles]
        total_load = total_load + jnp.where(owners[matrix] == me, 1.0, 0.0) * value
    halves[part] = jnp.full((8, 128), jnp.sum(total_load), F32)

    def half_copy(peer, place):
        return pltpu.make_async_remote_copy(
            src_ref=halves.at[place], dst_ref=halves.at[place],
            send_sem=half_send.at[peer], recv_sem=half_recv.at[place],
            device_id=(me, peer), device_id_type=MESH,
        )

    for step in range(1, parts):
        half_copy(lax.rem(part + step, parts), part).start()

    @pl.loop(0, 2)
    def _(slot):
        matrix = jnp.where(slot == 0, me - inner, singles + my_double)
        active = ((slot == 0) & has_single) | ((slot == 1) & has_double)
        place = jnp.where(slot == 0, matrix, matrix + upper * doubles)
        first = jnp.where(slot == 0, 0, upper * half)
        served = jnp.where(slot == 0, groups, half)

        @pl.when(active)
        def _():
            for step in range(1, parts):
                peer = lax.rem(part + step, parts)
                peer_copy(grams, slot, peer, part, gram_send, gram_recv).wait_send()
                peer_copy(traces, slot, peer, part, trace_send, trace_recv).wait_send()

            @pl.loop(0, served)
            def _(step):
                group = first + step
                elsewhere(group, lambda: result_copy(slot, group, matrix).wait_send())

            @pl.loop(1, groups)
            def _(step):
                load_copy(slot, group_at(step), place).wait_send()

            own_copy(slot, matrix).wait()

    @pl.loop(0, singles)
    def _(matrix):
        owner = single_owner(matrix)

        @pl.when(owner != me)
        def _():
            waited = ((me >= inner) & (me < groups - inner)) & (part == 0) & (lax.div(matrix, inner) != upper)
            waited = waited & (lax.rem(matrix - lax.rem(me, inner) + inner, inner) < inner)
            pl.when(jnp.logical_not(waited))(lambda: dir_copy(matrix, 0, 0, owner, me).wait_send())
            result_copy(0, me, matrix).wait_recv()

    @pl.loop(0, doubles)
    def _(index):
        matrix = singles + index
        for side in range(2):
            owner = double_owner(index, side)

            @pl.when(owner != me)
            def _():
                dir_copy(matrix, 1, side, owner, me).wait_send()

        elsewhere(
            double_owner(index, upper), lambda: result_copy(1, me, matrix).wait_recv()
        )

    for step in range(1, parts):
        peer = lax.rem(part + step, parts)
        half_copy(peer, part).wait_send()
        half_copy(peer, peer).wait_recv()
    owner_load[...] = jnp.sum(halves[...], axis=0) / (KV_OUT * D)
    mom_copy.wait()


def finish(
    update, momentum, load_block, norm_grads, norm_params, adam_m, adam_v,
    update_out, momentum_out, load_out, params_out, adam_m_out, adam_v_out,
    update_sem, momentum_sem,
):
    mats = momentum.shape[0]
    cuts = [mats * piece // 2 for piece in range(2 + 1)]
    copies = [
        pltpu.make_async_copy(
            source.at[pl.ds(start, stop - start)], target.at[pl.ds(start, stop - start)],
            sem.at[piece],
        )
        for source, target, sem in (
            (momentum, momentum_out, momentum_sem), (update, update_out, update_sem)
        )
        for piece, (start, stop) in enumerate(zip(cuts, cuts[1:]))
    ]
    for copy in copies:
        copy.start()
    grad = norm_grads[...]
    adam_m_new = adam_first * adam_m[...] + (1.0 - adam_first) * grad
    adam_v_new = adam_second * adam_v[...] + (1.0 - adam_second) * grad * grad
    corrected = adam_m_new / first_fix / (jnp.sqrt(adam_v_new / second_fix) + adam_eps)
    params_out[...] = norm_params[...] - adam_rate * corrected
    adam_m_out[...] = adam_m_new
    adam_v_out[...] = adam_v_new
    load_out[0] = load_block[0, 0]
    for copy in copies:
        copy.wait()


def on_device(groups, parts, grads, momentum, owners, norm_grads, norm_params, adam_m, adam_v):
    mats, rows, cols = grads.shape
    places = mats + (mats - groups // 2)
    dma = pltpu.SemaphoreType.DMA
    vmem = pl.BlockSpec(memory_space=pltpu.VMEM)
    hbm = pl.BlockSpec(memory_space=pl.ANY)
    update, momentum_new, load_block = pl.pallas_call(
        functools.partial(kernel, groups, parts, mats, 4),
        out_shape=(
            jax.ShapeDtypeStruct((mats, rows, cols), BF16),
            jax.ShapeDtypeStruct((mats, rows, cols), F32),
            jax.ShapeDtypeStruct((8, 128), F32),
        ),
        in_specs=[pl.BlockSpec(memory_space=pltpu.HBM)] * 3,
        out_specs=(hbm, hbm, vmem),
        scratch_shapes=[
            pltpu.VMEM((mats, rows, cols), BF16),
            pltpu.VMEM((2, groups, rows, cols), BF16),
            pltpu.VMEM((2, groups, rows, cols), BF16),
            pltpu.VMEM((2, parts, KV_OUT, KV_OUT), BF16),
            pltpu.VMEM((2, parts, 8, 128), F32),
            pltpu.VMEM((parts, 8, 128), F32),
            pltpu.VMEM((2, 8, 128), F32),
            pltpu.VMEM((places, 8, 128), F32),
            pltpu.VMEM((mats, rows, cols), F32),
            pltpu.VMEM((groups, rows, KV_OUT), BF16),
            dma((mats, 2)), dma((2, groups)), dma((2, groups)), dma((mats,)),
            dma((2, parts)), dma((2, parts)), dma((2, parts)), dma((2, parts)),
            dma((parts,)), dma((parts,)), dma((2, groups)), dma((places,)),
            dma((2,)), dma, pltpu.SemaphoreType.REGULAR, pltpu.SemaphoreType.REGULAR,
            pltpu.SMEM((mats,), jnp.int32),
            pltpu.VMEM((mats, rows, cols), BF16),
            pltpu.VMEM((mats, rows, cols), F32),
            dma, dma((mats,)), dma((mats,)),
        ],
        compiler_params=pltpu.CompilerParams(
            collective_id=0, has_side_effects=True, vmem_limit_bytes=28 * 1024 * 1024
        ),
    )(*(pltpu.with_memory_space_constraint(array, pltpu.HBM) for array in (owners, grads, momentum)))
    norm_shape = jax.ShapeDtypeStruct(norm_grads.shape, F32)
    update, momentum_new, owner_load, norm_params_new, adam_m_new, adam_v_new = pl.pallas_call(
        finish,
        out_shape=(
            jax.ShapeDtypeStruct(update.shape, BF16),
            jax.ShapeDtypeStruct(momentum_new.shape, F32),
            jax.ShapeDtypeStruct((1,), F32),
            norm_shape, norm_shape, norm_shape,
        ),
        in_specs=[hbm, hbm] + [vmem] * 5,
        out_specs=(
            pl.BlockSpec(memory_space=pltpu.HBM), pl.BlockSpec(memory_space=pltpu.HBM),
            pl.BlockSpec(memory_space=pltpu.SMEM), vmem, vmem, vmem,
        ),
        scratch_shapes=[dma((2,)), dma((2,))],
        compiler_params=pltpu.CompilerParams(vmem_limit_bytes=8 * 1024 * 1024),
    )(update, momentum_new, load_block, norm_grads, norm_params, adam_m, adam_v)
    return (update, momentum_new, owner_load, norm_params_new, adam_m_new, adam_v_new)


def solution(mesh):
    return jax.shard_map(
        functools.partial(on_device, mesh.shape["wide"], mesh.shape["narrow"]),
        mesh=mesh,
        in_specs=(
            P(None, "wide", "narrow"),
            P(None, "wide", "narrow"),
            P(),
            P("narrow", "wide"),
            P("narrow", "wide"),
            P("narrow", "wide"),
            P("narrow", "wide"),
        ),
        out_specs=(
            P(None, "wide", "narrow"),
            P(None, "wide", "narrow"),
            P("wide"),
            P("narrow", "wide"),
            P("narrow", "wide"),
            P("narrow", "wide"),
        ),
        check_vma=False,
    )
```

```python
import functools
import math

import jax
import jax.numpy as jnp
from jax import lax
from jax.experimental import pallas as pl
from jax.experimental.pallas import tpu as pltpu
from jax.sharding import PartitionSpec as P

D = 2048
KV_OUT = 512

coef_a = 3.4445
coef_b = -4.775
coef_c = 2.0315
muon_beta = 0.95
norm_eps = 1e-07
adam_first = 0.9
adam_second = 0.95
adam_rate = 0.02
adam_eps = 1e-08
first_fix = 1.0 - 0.9**10
second_fix = 1.0 - 0.95**10

MESH = pl.DeviceIdType.MESH
BF16 = jnp.bfloat16
F32 = jnp.float32


def mul(left, right):
    return jnp.dot(left, right, preferred_element_type=F32)


def kernel(
    groups, parts, mats, chunks,
    owners_hbm, grads_hbm, momentum_hbm,
    update, momentum_new, owner_load,
    dirs, blocks, results, grams, traces, halves, load_tile, loads, fresh, ident,
    dir_send, dir_recv, res_send, res_recv, gram_send, gram_recv,
    trace_send, trace_recv, half_send, half_recv, load_send, load_recv, own_sem, mom_sem, turn, ready,
    owners, grads, momentum, owners_sem, grads_sem, momentum_sem,
):
    me = lax.axis_index("wide")
    part = lax.axis_index("narrow")
    rows, cols = dirs.shape[1], dirs.shape[2]
    half = groups // 2
    inner = half // 2
    singles = half
    doubles = mats - singles
    upper = lax.div(me, half)

    def single_owner(matrix):
        return inner + matrix

    def double_owner(index, side):
        return jnp.where(side == 0, index, groups - 1 - index)

    my_double = jnp.where(upper == 0, me, groups - 1 - me)
    has_single = (me >= inner) & (me < inner + singles)
    has_double = my_double < doubles

    def group_at(step):
        return lax.rem(me + step, groups)

    def elsewhere(group, body):
        pl.when(group != me)(body)

    def loads_of(matrix):
        return (
            pltpu.make_async_copy(grads_hbm.at[matrix], grads.at[matrix], grads_sem.at[matrix]),
            pltpu.make_async_copy(
                momentum_hbm.at[matrix], momentum.at[matrix], momentum_sem.at[matrix]
            ),
        )

    def far_single(step):
        return (1 - upper) * inner + lax.rem(me + step, inner)

    def near_single(step):
        return upper * inner + lax.rem(me + step, inner)

    extra = doubles - inner

    def double_at(step):
        return jnp.where(
            step < inner, lax.rem(me + step, inner), inner + lax.rem(step + me, extra)
        )

    def fetch(matrix):
        for copy in loads_of(matrix):
            copy.start()

    owners_copy = pltpu.make_async_copy(owners_hbm, owners, owners_sem)
    barrier = pltpu.get_barrier_semaphore()
    outer = (me < inner) | (me >= groups - inner)

    def inner_at(step):
        return inner + lax.rem(lax.rem(me + inner, half) + step, half)

    @pl.loop(1, groups)
    def _(step):
        group = group_at(step)
        group_outer = (group < inner) | (group >= groups - inner)

        @pl.when(group_outer | jnp.logical_not(outer))
        def _():
            pl.semaphore_signal(barrier, inc=1, device_id=(group, part), device_id_type=MESH)

    for step in range(1, parts):
        peer = lax.rem(part + step, parts)
        pl.semaphore_signal(barrier, inc=1, device_id=(me, peer), device_id_type=MESH)

    @pl.loop(0, inner)
    def _(step):
        fetch(far_single(step))
        fetch(near_single(step))

    @pl.loop(0, doubles)
    def _(step):
        fetch(singles + double_at(step))


    owners_copy.start()

    def dir_copy(matrix, slot, which, group, source):
        return pltpu.make_async_remote_copy(
            src_ref=dirs.at[matrix], dst_ref=blocks.at[slot, source],
            send_sem=dir_send.at[matrix, which], recv_sem=dir_recv.at[slot, source],
            device_id=(group, part), device_id_type=MESH,
        )

    def direct(matrix):
        for copy in loads_of(matrix):
            copy.wait()
        grad_values = grads[matrix].astype(F32)
        new = muon_beta * momentum[matrix] + grad_values
        fresh[matrix] = new
        dirs[matrix] = (grad_values + muon_beta * new).astype(BF16)

    def send_single(matrix):
        owner = single_owner(matrix)
        elsewhere(owner, lambda: dir_copy(matrix, 0, 0, owner, me).start())

    def send_double(index, side):
        owner = double_owner(index, side)
        elsewhere(owner, lambda: dir_copy(singles + index, 1, side, owner, me).start())

    def pass_single(matrix):
        direct(matrix)
        send_single(matrix)

    def pass_double(index):
        direct(singles + index)
        pl.when(jnp.logical_not(((me >= inner) & (me < groups - inner)) & (part > 0)))(lambda: send_double(index, 1 - upper))
        pl.when(jnp.logical_not(((me >= inner) & (me < groups - inner)) & (part > 0)))(lambda: send_double(index, upper))

    @pl.when(outer)
    def _():
        pl.semaphore_wait(barrier, groups - 1 + parts - 1)

        @pl.loop(0, half)
        def _(step):
            pl.semaphore_signal(
                ready, inc=1, device_id=(inner_at(step), part), device_id_type=MESH
            )

    @pl.when(jnp.logical_not(outer))
    def _():
        pl.semaphore_wait(barrier, half - 1 + parts - 1)

    @pl.loop(0, inner)
    def _(step):
        pass_single(far_single(step))

    @pl.loop(0, inner)
    def _(step):
        pass_single(near_single(step))

    @pl.when(jnp.logical_not(outer))
    def _():
        pl.semaphore_wait(ready, half)

    @pl.loop(0, doubles)
    def _(step):
        pass_double(double_at(step))

    def single_sent(step):
        matrix = far_single(step)
        dir_copy(matrix, 0, 0, single_owner(matrix), me).wait_send()

    @pl.when((me >= inner) & (me < groups - inner))
    def _():
        @pl.when(part == 0)
        def _():
            @pl.loop(0, inner)
            def _(step):
                single_sent(step)

            for peer in range(1, parts):
                pl.semaphore_signal(turn, inc=1, device_id=(me, peer), device_id_type=MESH)

        @pl.when(part > 0)
        def _():
            pl.semaphore_wait(turn, 1)

            @pl.loop(0, doubles)
            def _(step):
                send_double(double_at(step), 1 - upper)
                send_double(double_at(step), upper)

    mom_copy = pltpu.make_async_copy(fresh, momentum_new, mom_sem)
    mom_copy.start()

    def result_copy(slot, group, matrix):
        return pltpu.make_async_remote_copy(
            src_ref=results.at[slot, group], dst_ref=update.at[matrix],
            send_sem=res_send.at[slot, group], recv_sem=res_recv.at[matrix],
            device_id=(group, part), device_id_type=MESH,
        )

    def own_copy(slot, matrix):
        return pltpu.make_async_copy(results.at[slot, me], update.at[matrix], own_sem.at[slot])

    def load_copy(slot, group, place):
        return pltpu.make_async_remote_copy(
            src_ref=load_tile.at[slot], dst_ref=loads.at[place],
            send_sem=load_send.at[slot, group], recv_sem=load_recv.at[place],
            device_id=(group, part), device_id_type=MESH,
        )

    def peer_copy(buffer, slot, peer, place, send, recv):
        return pltpu.make_async_remote_copy(
            src_ref=buffer.at[slot, place], dst_ref=buffer.at[slot, place],
            send_sem=send.at[slot, peer], recv_sem=recv.at[slot, place],
            device_id=(me, peer), device_id_type=MESH,
        )

    per_chunk = groups // chunks
    chunk_rows = KV_OUT // chunks

    @pl.loop(0, 2)
    def _(slot):
        matrix = jnp.where(slot == 0, me - inner, singles + my_double)
        active = ((slot == 0) & has_single) | ((slot == 1) & has_double)
        place = jnp.where(slot == 0, matrix, matrix + upper * doubles)
        served = jnp.where(slot == 0, groups, half)

        @pl.when(active)
        def _():
            blocks[slot, me] = dirs[matrix]
            row_ids = lax.broadcasted_iota(jnp.int32, (KV_OUT, KV_OUT), 0)
            col_ids = lax.broadcasted_iota(jnp.int32, (KV_OUT, KV_OUT), 1)

            @pl.loop(1, groups)
            def _(step):
                dir_copy(matrix, slot, 0, me, group_at(step)).wait_recv()

            whole = blocks[slot].reshape(KV_OUT, cols)
            partial_value = lax.dot_general(
                whole, whole, (((1,), (1,)), ((), ())), preferred_element_type=F32
            )
            grams[slot, part] = partial_value.astype(BF16)
            squares = jnp.sum(jnp.where(row_ids == col_ids, partial_value, 0.0))
            traces[slot, part] = jnp.full((8, 128), squares, F32)
            for step in range(1, parts):
                peer = lax.rem(part + step, parts)
                peer_copy(grams, slot, peer, part, gram_send, gram_recv).start()
                peer_copy(traces, slot, peer, part, trace_send, trace_recv).start()
            for step in range(1, parts):
                peer = lax.rem(part + step, parts)
                peer_copy(grams, slot, peer, peer, gram_send, gram_recv).wait_recv()
                peer_copy(traces, slot, peer, peer, trace_send, trace_recv).wait_recv()
            gram_sum = jnp.sum(grams[slot].astype(F32), axis=0)
            square_sum = jnp.sum(traces[slot], axis=0)[0:1, 0:1]
            scale = 1.0 / (jnp.sqrt(square_sum) + norm_eps)
            gram = (gram_sum * scale * scale).astype(BF16)
            gram_wide = gram.astype(F32)
            poly = coef_b * gram_wide + coef_c * mul(gram, gram)
            poly_first = poly.astype(BF16)
            mixed = mul(poly_first, gram)
            next_gram = (
                (coef_a * coef_a) * gram_wide
                + (2.0 * coef_a) * mixed
                + mul(mixed.astype(BF16), poly_first)
            ).astype(BF16)
            poly_second = (
                coef_b * next_gram.astype(F32) + coef_c * mul(next_gram, next_gram)
            )
            total = (
                coef_a * (poly_first.astype(F32) + poly_second)
                + mul(poly_second.astype(BF16), poly_first)
            )
            ident[...] = total.astype(BF16).reshape(ident.shape)
            out_scale = scale * math.sqrt(D)

            def chunk_at(step):
                forward = jnp.where(slot == 0, upper == 1, upper == 0)
                return jnp.where(forward, step, chunks - 1 - step)

            def send_chunk(first, start, stop):
                @pl.loop(start, stop)
                def _(member):
                    turned = jnp.where(first < half, per_chunk - member, member)
                    group = first + lax.rem(me + turned, per_chunk)
                    elsewhere(group, lambda: result_copy(slot, group, matrix).start())

                    @pl.when(group == me)
                    def _():
                        own_copy(slot, matrix).start()

            def chunk_body(step, square_total):
                first = chunk_at(step) * per_chunk
                mine = blocks[slot, pl.ds(first, per_chunk)].reshape(chunk_rows, cols)
                factor = ident[pl.ds(first, per_chunk)].reshape(chunk_rows, KV_OUT)
                values = (coef_a * coef_a) * mine.astype(F32) + mul(
                    factor, blocks[slot].reshape(KV_OUT, cols)
                )
                rounded = (out_scale * values).astype(BF16)
                results[slot, pl.ds(first, per_chunk)] = rounded.reshape(per_chunk, rows, cols)

                wide = rounded.astype(F32)
                squares = jnp.sum((wide * wide).reshape(chunk_rows // 8, 8, cols), axis=0)
                for lane in range(0, cols, 128):
                    square_total = square_total + squares[:, lane : lane + 128]

                @pl.when(step == last)
                def _():
                    load_tile[slot] = square_total
                    loads[place] = square_total

                    @pl.loop(1, groups)
                    def _(step):
                        load_copy(slot, group_at(step), place).start()

                    send_chunk(chunk_at(step - 1) * per_chunk, 0, per_chunk)

                send_chunk(first, 0, jnp.where(step == last - 1, 0, per_chunk))
                return square_total

            last = jnp.where(slot == 0, chunks, chunks // 2) - 1
            lax.fori_loop(0, last + 1, chunk_body, jnp.zeros((8, 128), F32))

    @pl.loop(0, singles)
    def _(matrix):
        elsewhere(single_owner(matrix), lambda: load_copy(0, me, matrix).wait_recv())

    @pl.loop(0, doubles)
    def _(index):
        for side in range(2):
            elsewhere(
                double_owner(index, side),
                lambda: load_copy(1, me, singles + index + side * doubles).wait_recv(),
            )

    owners_copy.wait()
    total_load = jnp.zeros((8, 128), F32)
    for matrix in range(mats):
        value = loads[matrix]
        if matrix >= singles:
            value = value + loads[matrix + doubles]
        total_load = total_load + jnp.where(owners[matrix] == me, 1.0, 0.0) * value
    halves[part] = jnp.full((8, 128), jnp.sum(total_load), F32)

    def half_copy(peer, place):
        return pltpu.make_async_remote_copy(
            src_ref=halves.at[place], dst_ref=halves.at[place],
            send_sem=half_send.at[peer], recv_sem=half_recv.at[place],
            device_id=(me, peer), device_id_type=MESH,
        )

    for step in range(1, parts):
        half_copy(lax.rem(part + step, parts), part).start()

    @pl.loop(0, 2)
    def _(slot):
        matrix = jnp.where(slot == 0, me - inner, singles + my_double)
        active = ((slot == 0) & has_single) | ((slot == 1) & has_double)
        place = jnp.where(slot == 0, matrix, matrix + upper * doubles)
        first = jnp.where(slot == 0, 0, upper * half)
        served = jnp.where(slot == 0, groups, half)

        @pl.when(active)
        def _():
            for step in range(1, parts):
                peer = lax.rem(part + step, parts)
                peer_copy(grams, slot, peer, part, gram_send, gram_recv).wait_send()
                peer_copy(traces, slot, peer, part, trace_send, trace_recv).wait_send()

            @pl.loop(0, served)
            def _(step):
                group = first + step
                elsewhere(group, lambda: result_copy(slot, group, matrix).wait_send())

            @pl.loop(1, groups)
            def _(step):
                load_copy(slot, group_at(step), place).wait_send()

            own_copy(slot, matrix).wait()

    @pl.loop(0, singles)
    def _(matrix):
        owner = single_owner(matrix)

        @pl.when(owner != me)
        def _():
            waited = ((me >= inner) & (me < groups - inner)) & (part == 0) & (lax.div(matrix, inner) != upper)
            waited = waited & (lax.rem(matrix - lax.rem(me, inner) + inner, inner) < inner)
            pl.when(jnp.logical_not(waited))(lambda: dir_copy(matrix, 0, 0, owner, me).wait_send())
            result_copy(0, me, matrix).wait_recv()

    @pl.loop(0, doubles)
    def _(index):
        matrix = singles + index
        for side in range(2):
            owner = double_owner(index, side)

            @pl.when(owner != me)
            def _():
                dir_copy(matrix, 1, side, owner, me).wait_send()

        elsewhere(
            double_owner(index, upper), lambda: result_copy(1, me, matrix).wait_recv()
        )

    for step in range(1, parts):
        peer = lax.rem(part + step, parts)
        half_copy(peer, part).wait_send()
        half_copy(peer, peer).wait_recv()
    owner_load[...] = jnp.sum(halves[...], axis=0) / (KV_OUT * D)
    mom_copy.wait()


def finish(
    update, momentum, load_block, norm_grads, norm_params, adam_m, adam_v,
    update_out, momentum_out, load_out, params_out, adam_m_out, adam_v_out,
    update_sem, momentum_sem,
):
    mats = momentum.shape[0]
    cuts = [mats * piece // 2 for piece in range(2 + 1)]
    copies = [
        pltpu.make_async_copy(
            source.at[pl.ds(start, stop - start)], target.at[pl.ds(start, stop - start)],
            sem.at[piece],
        )
        for source, target, sem in (
            (momentum, momentum_out, momentum_sem), (update, update_out, update_sem)
        )
        for piece, (start, stop) in enumerate(zip(cuts, cuts[1:]))
    ]
    for copy in copies:
        copy.start()
    grad = norm_grads[...]
    adam_m_new = adam_first * adam_m[...] + (1.0 - adam_first) * grad
    adam_v_new = adam_second * adam_v[...] + (1.0 - adam_second) * grad * grad
    corrected = adam_m_new / first_fix / (jnp.sqrt(adam_v_new / second_fix) + adam_eps)
    params_out[...] = norm_params[...] - adam_rate * corrected
    adam_m_out[...] = adam_m_new
    adam_v_out[...] = adam_v_new
    load_out[0] = load_block[0, 0]
    for copy in copies:
        copy.wait()


def on_device(groups, parts, grads, momentum, owners, norm_grads, norm_params, adam_m, adam_v):
    mats, rows, cols = grads.shape
    places = mats + (mats - groups // 2)
    dma = pltpu.SemaphoreType.DMA
    vmem = pl.BlockSpec(memory_space=pltpu.VMEM)
    hbm = pl.BlockSpec(memory_space=pl.ANY)
    update, momentum_new, load_block = pl.pallas_call(
        functools.partial(kernel, groups, parts, mats, 4),
        out_shape=(
            jax.ShapeDtypeStruct((mats, rows, cols), BF16),
            jax.ShapeDtypeStruct((mats, rows, cols), F32),
            jax.ShapeDtypeStruct((8, 128), F32),
        ),
        in_specs=[pl.BlockSpec(memory_space=pltpu.HBM)] * 3,
        out_specs=(hbm, hbm, vmem),
        scratch_shapes=[
            pltpu.VMEM((mats, rows, cols), BF16),
            pltpu.VMEM((2, groups, rows, cols), BF16),
            pltpu.VMEM((2, groups, rows, cols), BF16),
            pltpu.VMEM((2, parts, KV_OUT, KV_OUT), BF16),
            pltpu.VMEM((2, parts, 8, 128), F32),
            pltpu.VMEM((parts, 8, 128), F32),
            pltpu.VMEM((2, 8, 128), F32),
            pltpu.VMEM((places, 8, 128), F32),
            pltpu.VMEM((mats, rows, cols), F32),
            pltpu.VMEM((groups, rows, KV_OUT), BF16),
            dma((mats, 2)), dma((2, groups)), dma((2, groups)), dma((mats,)),
            dma((2, parts)), dma((2, parts)), dma((2, parts)), dma((2, parts)),
            dma((parts,)), dma((parts,)), dma((2, groups)), dma((places,)),
            dma((2,)), dma, pltpu.SemaphoreType.REGULAR, pltpu.SemaphoreType.REGULAR,
            pltpu.SMEM((mats,), jnp.int32),
            pltpu.VMEM((mats, rows, cols), BF16),
            pltpu.VMEM((mats, rows, cols), F32),
            dma, dma((mats,)), dma((mats,)),
        ],
        compiler_params=pltpu.CompilerParams(
            collective_id=0, has_side_effects=True, vmem_limit_bytes=28 * 1024 * 1024
        ),
    )(*(pltpu.with_memory_space_constraint(array, pltpu.HBM) for array in (owners, grads, momentum)))
    norm_shape = jax.ShapeDtypeStruct(norm_grads.shape, F32)
    update, momentum_new, owner_load, norm_params_new, adam_m_new, adam_v_new = pl.pallas_call(
        finish,
        out_shape=(
            jax.ShapeDtypeStruct(update.shape, BF16),
            jax.ShapeDtypeStruct(momentum_new.shape, F32),
            jax.ShapeDtypeStruct((1,), F32),
            norm_shape, norm_shape, norm_shape,
        ),
        in_specs=[hbm, hbm] + [vmem] * 5,
        out_specs=(
            pl.BlockSpec(memory_space=pltpu.HBM), pl.BlockSpec(memory_space=pltpu.HBM),
            pl.BlockSpec(memory_space=pltpu.SMEM), vmem, vmem, vmem,
        ),
        scratch_shapes=[dma((2,)), dma((2,))],
        compiler_params=pltpu.CompilerParams(vmem_limit_bytes=8 * 1024 * 1024),
    )(update, momentum_new, load_block, norm_grads, norm_params, adam_m, adam_v)
    return (update, momentum_new, owner_load, norm_params_new, adam_m_new, adam_v_new)


def solution(mesh):
    return jax.shard_map(
        functools.partial(on_device, mesh.shape["wide"], mesh.shape["narrow"]),
        mesh=mesh,
        in_specs=(
            P(None, "wide", "narrow"),
            P(None, "wide", "narrow"),
            P(),
            P("narrow", "wide"),
            P("narrow", "wide"),
            P("narrow", "wide"),
            P("narrow", "wide"),
        ),
        out_specs=(
            P(None, "wide", "narrow"),
            P(None, "wide", "narrow"),
            P("wide"),
            P("narrow", "wide"),
            P("narrow", "wide"),
            P("narrow", "wide"),
        ),
        check_vma=False,
    )
```
